32 devices in a mesh: seq: 8 (over z, core), head: 4 (over y, x).
Axes of the slice: x: 2, y: 2, z: 4, core: 2. Of those that a mesh axis runs over, the one named last changes fastest.
Arguments:
- video_query: bfloat16 [4096, 3072], P(('seq', 'head')), may hold values from -8 to 8
- video_key: bfloat16 [4096, 3072], P(('seq', 'head')), may hold values from -8 to 8
- video_value: bfloat16 [4096, 3072], P(('seq', 'head')), may hold values from -6 to 6
- video_grad: bfloat16 [4096, 3072], P(('seq', 'head')), may hold values from -6 to 6
- text_query: bfloat16 [256, 3072], P(None, 'head'), may hold values from -8 to 8
- text_key: bfloat16 [256, 3072], P(None, 'head'), may hold values from -8 to 8
- text_value: bfloat16 [256, 3072], P(None, 'head'), may hold values from -6 to 6
- text_grad: bfloat16 [256, 3072], P(None, 'head'), may hold values from -6 to 6
- tile_list: int32 [32, 8], replicated, may hold values from 0 to 31, as said below
- tile_count: int32 [32], replicated, may hold values from 1 to 8, as said below
- text_mask: int32 [256], replicated, may hold values from 0 to 1, as said below
Outputs:
- attended_video: bfloat16 [4096, 3072], P(('seq', 'head'))
- video_query_grad: bfloat16 [4096, 3072], P(('seq', 'head'))
- video_key_grad: bfloat16 [4096, 3072], P(('seq', 'head'))
- video_value_grad: bfloat16 [4096, 3072], P(('seq', 'head'))
- attended_text: bfloat16 [256, 3072], P(None, 'head')
- text_query_grad: bfloat16 [256, 3072], P(None, 'head')
- text_key_grad: bfloat16 [256, 3072], P(None, 'head')
- text_value_grad: bfloat16 [256, 3072], P(None, 'head')
The draws below stay inside these ranges and needn't reach their ends.
Inputs may be any that keep to these rules, and one draw needn't show every extreme that they name: `tile_list`: the 8 entries of one query tile's list are distinct. Query tiles fall in aligned blocks of 4; the used entries of one block together name at most 2 distinct tiles of any other block of 4 tiles, and every block names exactly 2 from some other block. `tile_count`: every aligned block of 4 query tiles has a tile that uses all 8 entries. `text_mask`: the ones form a prefix of at least 64 entries.
All inputs are finite; a program needn't handle non-finite values.
Results may differ from the reference program's by a relative error of at most 0.012.
Values may be sent and summed in bfloat16 or wider, within the bound.
A program may use at most 192 MiB of HBM per device.

```python
from functools import partial
import jax
import jax.numpy as jnp
from jax import lax

H = 24
HD = 128
D = 3072
TXT = 256
TILE = 128
KT = 8
MOST = 2
VID = 4096
QT = 32
TPS = 4


def drawn_rows(key, own_key, row_total):
    normal_part = jax.random.normal(jax.random.fold_in(own_key, 17), (row_total, D), jnp.float32)
    normal_part = jnp.clip(normal_part, -8.0, 8.0)
    return normal_part


def draw_video_query(key, part):
    return drawn_rows(key, jax.random.fold_in(key, 101), VID).astype(jnp.bfloat16)


def draw_text_query(key, part):
    return drawn_rows(key, jax.random.fold_in(key, 202), TXT).astype(jnp.bfloat16)


def draw_video_key(key, part):
    own_key = jax.random.fold_in(key, 404)
    normal_part = jax.random.normal(own_key, (VID, D), jnp.float32)
    normal_part = jnp.clip(normal_part, -6.0, 6.0)
    return normal_part.astype(jnp.bfloat16)


def draw_text_key(key, part):
    own_key = jax.random.fold_in(key, 303)
    normal_part = jnp.clip(jax.random.normal(own_key, (TXT, D), jnp.float32), -8.0, 8.0)
    return normal_part.astype(jnp.bfloat16)


def tile_plan(key):
    key = jax.random.fold_in(key, 4242)
    groups = QT // TPS
    width_all = TPS + groups * MOST
    keys_split = jax.random.split(key, 5)
    raw = jax.random.randint(keys_split[0], (groups, groups, TPS), 0, 1 << 20)
    order = jnp.argsort(raw * TPS + jnp.arange(TPS), axis=-1)
    offered = order[:, :, :MOST] + (jnp.arange(groups) * TPS)[None, :, None]
    local_tiles = (jnp.arange(groups) * TPS)[:, None] + jnp.arange(TPS)[None, :]
    pool = jnp.concatenate([local_tiles, offered.reshape(groups, groups * MOST)], axis=1)
    source = jnp.concatenate([jnp.broadcast_to(jnp.arange(groups)[:, None], (groups, TPS)), jnp.broadcast_to(jnp.arange(groups)[None, :, None], (groups, groups, MOST)).reshape(groups, groups * MOST)], axis=1)
    is_slot = jnp.arange(width_all) >= TPS
    usable = jnp.logical_not(is_slot[None, :] & (source == jnp.arange(groups)[:, None]))
    chosen_tile = jax.random.randint(keys_split[1], (groups,), 0, TPS)
    chosen_source = (jnp.arange(groups) + jax.random.randint(keys_split[2], (groups,), 1, groups)) % groups
    scores = jax.random.randint(keys_split[3], (groups, TPS, width_all), 0, 1 << 12) * width_all + jnp.arange(width_all)
    forced = (jnp.arange(TPS)[None, :, None] == chosen_tile[:, None, None]) & (source[:, None, :] == chosen_source[:, None, None]) & is_slot[None, None, :]
    scores = jnp.where(forced, jnp.arange(width_all) - width_all, scores)
    scores = jnp.where(usable[:, None, :], scores, (1 << 12) * width_all + jnp.arange(width_all))
    picked = jnp.argsort(scores, axis=-1)[:, :, :KT]
    lists = jnp.take_along_axis(jnp.broadcast_to(pool[:, None, :], (groups, TPS, width_all)), picked, axis=-1).reshape(QT, KT)
    counts = jax.random.randint(keys_split[4], (groups, TPS), 1, KT + 1)
    counts = jnp.where(jnp.arange(TPS)[None, :] == chosen_tile[:, None], KT, counts).reshape(QT)
    return (lists.astype(jnp.int32), counts.astype(jnp.int32))


def draw_tile_list(key, part):
    return tile_plan(key)[0]


def draw_tile_count(key, part):
    return tile_plan(key)[1]


def draw_text_mask(key, part):
    keep = jax.random.randint(jax.random.fold_in(key, 505), (), TXT // 4, TXT + 1)
    return (jnp.arange(TXT) < keep).astype(jnp.int32)


def block_scale(stream_key, extent, cuts, low, largest):
    gain, own = 1.0, jax.random.fold_in(stream_key, 6)
    for dim, shards_of in cuts:
        steps = jnp.exp(jax.random.uniform(jax.random.fold_in(own, dim), (shards_of,), jnp.float32, low / len(cuts), largest / len(cuts)))
        gain = gain * jnp.repeat(steps, extent[dim] // shards_of).reshape([-1 if axis == dim else 1 for axis in range(len(extent))])
    return gain


def bell_draw(rng, shape, deviation, most, pieces=(), held_as=jnp.bfloat16):
    result = deviation * jax.random.normal(rng, shape, jnp.float32)
    if pieces:
        result = result * block_scale(rng, shape, pieces, -0.22, 0.18)
    return jnp.clip(result, -most, most).astype(held_as)


def setup_inputs(seed: int = 0) -> dict:
    splits = jax.random.split(jax.random.key(seed), 12)
    video_query = draw_video_query(jax.random.fold_in(splits[11], 71), 0)
    video_key = draw_video_key(jax.random.fold_in(splits[11], 71), 0)
    video_value = bell_draw(splits[2], (VID, D), 1.0, 6.0, ((0, 32),))
    video_grad = bell_draw(splits[3], (VID, D), 1.0, 6.0, ((0, 32),))
    text_query = draw_text_query(jax.random.fold_in(splits[11], 71), 0)
    text_key = draw_text_key(jax.random.fold_in(splits[11], 71), 0)
    text_value = bell_draw(splits[6], (TXT, D), 1.0, 6.0, ((1, 4),))
    text_grad = bell_draw(splits[7], (TXT, D), 1.0, 6.0, ((1, 4),))
    tile_list = draw_tile_list(jax.random.fold_in(splits[11], 71), 0)
    tile_count = draw_tile_count(jax.random.fold_in(splits[11], 71), 0)
    text_mask = draw_text_mask(jax.random.fold_in(splits[11], 71), 0)
    return dict(video_query=video_query, video_key=video_key, video_value=video_value, video_grad=video_grad, text_query=text_query, text_key=text_key, text_value=text_value, text_grad=text_grad, tile_list=tile_list, tile_count=tile_count, text_mask=text_mask)


NEGATIVE = -1.0e30
HIGHEST_PRECISION = lax.Precision.HIGHEST


def per_head(arrays, tile_list, tile_count, text_ok):
    query_vid, key_vid, value_vid, grad_vid, query_txt, key_txt, value_txt, grad_txt = arrays
    factor = HD ** -0.5
    key_tiles = key_vid.reshape(QT, TILE, HD)
    value_tiles = value_vid.reshape(QT, TILE, HD)

    def step(running, tile_index):
        key_acc, value_acc, text_key_acc, text_value_acc = running
        query_rows = lax.dynamic_slice_in_dim(query_vid, tile_index * TILE, TILE, 0)
        grad_rows = lax.dynamic_slice_in_dim(grad_vid, tile_index * TILE, TILE, 0)
        listed = tile_list[tile_index]
        key_rows = jnp.concatenate([key_tiles[listed].reshape(KT * TILE, HD), key_txt], axis=0)
        value_rows = jnp.concatenate([value_tiles[listed].reshape(KT * TILE, HD), value_txt], axis=0)
        live_keys = jnp.concatenate([jnp.repeat(jnp.arange(KT) < tile_count[tile_index], TILE), text_ok])
        scores = jnp.dot(query_rows, key_rows.T, preferred_element_type=jnp.float32) * factor
        scores = jnp.where(live_keys[None, :], scores, NEGATIVE)
        maximum = jnp.max(scores, axis=1, keepdims=True)
        log_total = maximum + jnp.log(jnp.sum(jnp.exp(scores - maximum), axis=1, keepdims=True))
        probability = jnp.exp(scores - log_total)
        weights = probability.astype(jnp.bfloat16)
        output = jnp.dot(weights, value_rows, preferred_element_type=jnp.float32)
        offset = jnp.sum(grad_rows.astype(jnp.float32) * output, axis=1, keepdims=True)
        prob_grad = jnp.dot(grad_rows, value_rows.T, preferred_element_type=jnp.float32)
        score_grad = (probability * (prob_grad - offset)).astype(jnp.bfloat16)
        query_grad = jnp.dot(score_grad, key_rows, preferred_element_type=jnp.float32) * factor
        key_grad = jnp.dot(score_grad.T, query_rows, preferred_element_type=jnp.float32) * factor
        value_grad = jnp.dot(weights.T, grad_rows, preferred_element_type=jnp.float32)
        key_acc = key_acc.at[listed].add(key_grad[:KT * TILE].reshape(KT, TILE, HD))
        value_acc = value_acc.at[listed].add(value_grad[:KT * TILE].reshape(KT, TILE, HD))
        text_key_acc = text_key_acc + key_grad[KT * TILE:]
        text_value_acc = text_value_acc + value_grad[KT * TILE:]
        return (key_acc, value_acc, text_key_acc, text_value_acc), (output.astype(jnp.bfloat16), query_grad.astype(jnp.bfloat16))

    start = (jnp.zeros((QT, TILE, HD), jnp.float32), jnp.zeros((QT, TILE, HD), jnp.float32),
             jnp.zeros((TXT, HD), jnp.float32), jnp.zeros((TXT, HD), jnp.float32))
    finals, outputs = lax.scan(step, start, jnp.arange(QT, dtype=jnp.int32))
    key_acc, value_acc, text_key_acc, text_value_acc = finals
    video_out = outputs[0].reshape(VID, HD)
    video_query_grad = outputs[1].reshape(VID, HD)

    key_all = jnp.concatenate([key_vid, key_txt], axis=0)
    value_all = jnp.concatenate([value_vid, value_txt], axis=0)
    live_all = jnp.concatenate([jnp.ones((VID,), bool), text_ok])
    scores = jnp.dot(query_txt, key_all.T, preferred_element_type=jnp.float32) * factor
    scores = jnp.where(live_all[None, :], scores, NEGATIVE)
    maximum = jnp.max(scores, axis=1, keepdims=True)
    log_total = maximum + jnp.log(jnp.sum(jnp.exp(scores - maximum), axis=1, keepdims=True))
    probability = jnp.exp(scores - log_total)
    text_out = jnp.dot(probability, value_all.astype(jnp.float32), precision=HIGHEST_PRECISION)
    offset = jnp.sum(grad_txt.astype(jnp.float32) * text_out, axis=1, keepdims=True)
    prob_grad = jnp.dot(grad_txt, value_all.T, preferred_element_type=jnp.float32)
    score_grad = probability * (prob_grad - offset)
    text_query_grad = jnp.dot(score_grad, key_all.astype(jnp.float32), precision=HIGHEST_PRECISION) * factor
    key_from_text = jnp.dot(score_grad.T, query_txt.astype(jnp.float32), precision=HIGHEST_PRECISION) * factor
    value_from_text = jnp.dot(probability.T, grad_txt.astype(jnp.float32), precision=HIGHEST_PRECISION)
    video_key_grad = key_acc.reshape(VID, HD) + key_from_text[:VID]
    video_value_grad = value_acc.reshape(VID, HD) + value_from_text[:VID]
    text_key_grad = text_key_acc + key_from_text[VID:]
    text_value_grad = text_value_acc + value_from_text[VID:]
    return (video_out, video_query_grad, video_key_grad.astype(jnp.bfloat16), video_value_grad.astype(jnp.bfloat16),
            text_out.astype(jnp.bfloat16), text_query_grad.astype(jnp.bfloat16),
            text_key_grad.astype(jnp.bfloat16), text_value_grad.astype(jnp.bfloat16))


def split_heads(matrix):
    return jnp.transpose(matrix.reshape(matrix.shape[0], H, HD), (1, 0, 2))


def join_heads(matrix):
    return jnp.transpose(matrix, (1, 0, 2)).reshape(matrix.shape[1], H * HD)


def reference(video_query, video_key, video_value, video_grad, text_query, text_key, text_value, text_grad, tile_list, tile_count, text_mask):
    text_ok = text_mask > 0
    stacked = tuple(split_heads(matrix) for matrix in (video_query, video_key, video_value, video_grad, text_query, text_key, text_value, text_grad))
    results = lax.map(partial(per_head, tile_list=tile_list, tile_count=tile_count, text_ok=text_ok), stacked)
    return (join_heads(results[0]), join_heads(results[1]), join_heads(results[2]), join_heads(results[3]),
            join_heads(results[4]), join_heads(results[5]), join_heads(results[6]), join_heads(results[7]))
```

```python
import functools

import jax
import jax.numpy as jnp
from jax import lax
from jax.experimental import pallas as pl
from jax.experimental.pallas import tpu as pltpu
from jax.sharding import Mesh, PartitionSpec as P

HD = 128
TILE = 128
NEGATIVE = -1e30
LOG2E = 1.4426950408889634
FACTOR = HD**-0.5


def dot_nt(a, b):
    return lax.dot_general(a, b, (((1,), (1,)), ((), ())), preferred_element_type=jnp.float32)


def dot_tn(a, b):
    return lax.dot_general(a, b, (((0,), (0,)), ((), ())), preferred_element_type=jnp.float32)


def dot_nn(a, b):
    return lax.dot_general(a, b, (((1,), (0,)), ((), ())), preferred_element_type=jnp.float32)


def attend_kernel(
    outer,
    entries,
    slot_ref,
    count_ref,
    q_ref,
    g_ref,
    k_ref,
    v_ref,
    tq_ref,
    tg_ref,
    tk_ref,
    tv_ref,
    bias_ref,
    o_ref,
    dq_ref,
    dk_ref,
    dv_ref,
    to_ref,
    tdq_ref,
    kbuf,
    vbuf,
    sbuf,
    dk_acc,
    dv_acc,
):
    video = k_ref.shape[0]
    text = tk_ref.shape[0]
    chunk = q_ref.shape[0]
    part = tq_ref.shape[0]
    listed = entries * TILE
    scale2 = FACTOR * LOG2E
    kbuf[pl.ds(listed, text), :] = tk_ref[...]
    vbuf[pl.ds(listed, text), :] = tv_ref[...]

    block = 512
    steps = video // block
    tq = tq_ref[...]
    tg = tg_ref[...]
    text_s = dot_nt(tk_ref[...], tq) * scale2 + bias_ref[:, :part]
    top = jnp.max(text_s, axis=0, keepdims=True)

    def scores(i, top):
        rows = pl.ds(pl.multiple_of(i * block, block), block)
        s = dot_nt(k_ref[rows, :], tq) * scale2
        sbuf[rows, :] = s
        return jnp.maximum(top, jnp.max(s, axis=0, keepdims=True))

    top = lax.fori_loop(0, steps, scores, top)
    text_e = jnp.exp2(text_s - top)

    def weigh(i, carry):
        total, out = carry
        rows = pl.ds(pl.multiple_of(i * block, block), block)
        e = jnp.exp2(sbuf[rows, :] - top)
        sbuf[rows, :] = e
        out = out + dot_tn(e.astype(jnp.bfloat16), v_ref[rows, :])
        return total + jnp.sum(e, axis=0, keepdims=True), out

    total, out = lax.fori_loop(
        0,
        steps,
        weigh,
        (
            jnp.sum(text_e, axis=0, keepdims=True),
            dot_tn(text_e.astype(jnp.bfloat16), tv_ref[...]),
        ),
    )
    inverse = 1.0 / total
    out = out * jnp.transpose(inverse)
    to_ref[...] = out.astype(jnp.bfloat16)
    delta = jnp.transpose(jnp.sum(tg.astype(jnp.float32) * out, axis=1, keepdims=True))

    def spread(e, key, value):
        p = e * inverse
        dv = dot_nn(p.astype(jnp.bfloat16), tg)
        ds = (p * (dot_nt(value, tg) - delta)).astype(jnp.bfloat16)
        return dot_nn(ds, tq), dv, dot_tn(ds, key)

    dk, dv, dq = spread(text_e, tk_ref[...], tv_ref[...])
    dk_acc[pl.ds(video, text), :] = dk
    dv_acc[pl.ds(video, text), :] = dv

    def back(i, dq):
        rows = pl.ds(pl.multiple_of(i * block, block), block)
        dk, dv, more = spread(sbuf[rows, :], k_ref[rows, :], v_ref[rows, :])
        dk_acc[rows, :] = dk
        dv_acc[rows, :] = dv
        return dq + more

    dq = lax.fori_loop(0, steps, back, dq)
    tdq_ref[...] = (dq * FACTOR).astype(jnp.bfloat16)

    def tile(i, carry):
        rows = pl.ds(pl.multiple_of(i * TILE, TILE), TILE)
        spots = [
            pl.ds(pl.multiple_of(slot_ref[i * entries + e] * TILE, TILE), TILE)
            for e in range(entries)
        ]
        count = count_ref[i]
        q = q_ref[rows, :]
        g = g_ref[rows, :]
        for e in range(entries):
            kbuf[pl.ds(e * TILE, TILE), :] = k_ref[spots[e], :]
            vbuf[pl.ds(e * TILE, TILE), :] = v_ref[spots[e], :]
        keys = kbuf[...]
        values = vbuf[...]
        s = dot_nt(keys, q) * scale2
        parts = [
            s[e * TILE : (e + 1) * TILE] + jnp.where(e < count, 0.0, NEGATIVE)
            for e in range(entries)
        ]
        s = jnp.concatenate(parts + [s[listed:] + bias_ref[...]], axis=0)
        e = jnp.exp2(s - jnp.max(s, axis=0, keepdims=True))
        p = e * (1.0 / jnp.sum(e, axis=0, keepdims=True))
        weights = p.astype(jnp.bfloat16)
        out = dot_tn(weights, values)
        o_ref[rows, :] = out.astype(jnp.bfloat16)
        delta = jnp.transpose(jnp.sum(g.astype(jnp.float32) * out, axis=1, keepdims=True))
        ds = (p * (dot_nt(values, g) - delta)).astype(jnp.bfloat16)
        dq_ref[rows, :] = (dot_tn(ds, keys) * FACTOR).astype(jnp.bfloat16)
        dk = dot_nn(ds, q)
        dv = dot_nn(weights, g)
        for e in range(entries):
            dk_acc[spots[e], :] += dk[e * TILE : (e + 1) * TILE]
            dv_acc[spots[e], :] += dv[e * TILE : (e + 1) * TILE]
        dk_acc[pl.ds(video, text), :] += dk[listed:]
        dv_acc[pl.ds(video, text), :] += dv[listed:]
        return carry

    lax.fori_loop(0, chunk // TILE, tile, 0)

    for z in range(outer):
        at = z * (chunk + part)
        dk_ref[pl.ds(at, chunk), :] = (dk_acc[pl.ds(z * chunk, chunk), :] * FACTOR).astype(
            dk_ref.dtype
        )
        dv_ref[pl.ds(at, chunk), :] = dv_acc[pl.ds(z * chunk, chunk), :].astype(dv_ref.dtype)
        dk_ref[pl.ds(at + chunk, part), :] = (
            dk_acc[pl.ds(video + z * part, part), :] * FACTOR
        ).astype(dk_ref.dtype)
        dv_ref[pl.ds(at + chunk, part), :] = dv_acc[pl.ds(video + z * part, part), :].astype(
            dv_ref.dtype
        )


def attend(outer, slots, counts, q, g, k, v, tq, tg, tk, tv, bias):
    chunk, width = q.shape
    video = k.shape[0]
    text = tk.shape[0]
    part = tq.shape[0]
    entries = slots.shape[1]
    rows = lambda n: pl.BlockSpec((n, HD), lambda h, *_: (0, h))
    total = video + text
    call = pl.pallas_call(
        functools.partial(attend_kernel, outer, entries),
        grid_spec=pltpu.PrefetchScalarGridSpec(
            num_scalar_prefetch=2,
            grid=(width // HD,),
            in_specs=[
                rows(chunk),
                rows(chunk),
                rows(video),
                rows(video),
                rows(part),
                rows(part),
                rows(text),
                rows(text),
                pl.BlockSpec((text, TILE), lambda h, *_: (0, 0)),
            ],
            out_specs=[
                rows(chunk),
                rows(chunk),
                rows(total),
                rows(total),
                rows(part),
                rows(part),
            ],
            scratch_shapes=[
                pltpu.VMEM((entries * TILE + text, HD), jnp.bfloat16),
                pltpu.VMEM((entries * TILE + text, HD), jnp.bfloat16),
                pltpu.VMEM((video, part), jnp.float32),
                pltpu.VMEM((total, HD), jnp.float32),
                pltpu.VMEM((total, HD), jnp.float32),
            ],
        ),
        out_shape=[
            jax.ShapeDtypeStruct((chunk, width), jnp.bfloat16),
            jax.ShapeDtypeStruct((chunk, width), jnp.bfloat16),
            jax.ShapeDtypeStruct((total, width), jnp.bfloat16),
            jax.ShapeDtypeStruct((total, width), jnp.bfloat16),
            jax.ShapeDtypeStruct((part, width), jnp.bfloat16),
            jax.ShapeDtypeStruct((part, width), jnp.bfloat16),
        ],
        compiler_params=pltpu.CompilerParams(vmem_limit_bytes=63 * 1024 * 1024),
        name="attend",
    )
    return call(slots.reshape(-1), counts, q, g, k, v, tq, tg, tk, tv, bias)


def body(
    video_query,
    video_key,
    video_value,
    video_grad,
    text_query,
    text_key,
    text_value,
    text_grad,
    tile_list,
    tile_count,
    text_mask,
):
    outer, core, head = (lax.axis_size(name) for name in ("outer", "core", "head"))
    own, own_core = lax.axis_index("outer"), lax.axis_index("core")
    near = ("head", "core")
    rows, width = video_query.shape
    feat = width // (head * core)
    text = text_query.shape[0]
    part = text // outer
    tiles = rows // TILE

    def to_heads(x):
        return lax.all_to_all(x, near, split_axis=1, concat_axis=0, tiled=True)

    def to_tokens(x):
        return lax.all_to_all(x, near, split_axis=0, concat_axis=1, tiled=True)

    keys = lax.all_gather(to_heads(video_key), "outer", axis=0, tiled=True)
    values = lax.all_gather(to_heads(video_value), "outer", axis=0, tiled=True)
    queries = to_heads(video_query)
    grads = to_heads(video_grad)
    chunk = queries.shape[0]

    block = tile_list // tiles
    spot = ((block // head) % core) + (block % head) * core
    slot = (block // (head * core)) * (chunk // TILE) + spot * tiles + tile_list % tiles
    place = jnp.arange(chunk // TILE)
    mine = place // tiles
    mine = (own * core + mine % core) * head + mine // core
    mine = mine * tiles + place % tiles
    slots = slot[mine].astype(jnp.int32)
    counts = tile_count[mine].astype(jnp.int32)
    bias = jnp.broadcast_to(
        jnp.where(text_mask > 0, 0.0, NEGATIVE).astype(jnp.float32)[:, None], (text, TILE)
    )

    mine_of = lambda x: lax.dynamic_slice_in_dim(x, own_core * feat, feat, 1)
    part_of = lambda x: lax.dynamic_slice_in_dim(x, own * part, part, 0)
    tk, tv, tq, tg = (mine_of(x) for x in (text_key, text_value, text_query, text_grad))
    o, dq, dk, dv, to, tdq = attend(
        outer, slots, counts, queries, grads, keys, values, part_of(tq), part_of(tg), tk, tv, bias
    )
    attended = to_tokens(o)
    query_grad = to_tokens(dq)
    dk = lax.psum_scatter(dk, "outer", scatter_dimension=0, tiled=True)
    dv = lax.psum_scatter(dv, "outer", scatter_dimension=0, tiled=True)
    key_grad = to_tokens(dk[:chunk])
    value_grad = to_tokens(dv[:chunk])
    texts = jnp.stack([to, tdq, dk[chunk:], dv[chunk:]])
    texts = lax.all_gather(texts, ("outer", "core"), axis=0, tiled=False)
    texts = texts.reshape(outer, core, 4, part, feat).transpose(2, 0, 3, 1, 4)
    texts = texts.reshape(4, text, core * feat)
    return (attended, query_grad, key_grad, value_grad, texts[0], texts[1], texts[2], texts[3])


def solution(mesh):
    seq, head = mesh.shape["seq"], mesh.shape["head"]
    video = P(("outer", "core", "head"), None)
    side = P(None, "head")

    def run(*arrays):
        heads = arrays[0].shape[1] // HD // head
        core = 2 if heads % 2 == 0 and seq % 2 == 0 else 1
        grid = Mesh(mesh.devices.reshape(seq // core, core, head), ("outer", "core", "head"))
        return jax.shard_map(
            body,
            mesh=grid,
            in_specs=(video,) * 4 + (side,) * 4 + (P(), P(), P()),
            out_specs=(video,) * 4 + (side,) * 4,
            check_vma=False,
        )(*arrays)

    return run
```

```python
import functools

import jax
import jax.numpy as jnp
from jax import lax
from jax.experimental import pallas as pl
from jax.experimental.pallas import tpu as pltpu
from jax.sharding import PartitionSpec as P

HD = 128
TILE = 128
NEGATIVE = -1e30
LOG2E = 1.4426950408889634
FACTOR = HD**-0.5


def dot_nt(a, b):
    return lax.dot_general(a, b, (((1,), (1,)), ((), ())), preferred_element_type=jnp.float32)


def dot_tn(a, b):
    return lax.dot_general(a, b, (((0,), (0,)), ((), ())), preferred_element_type=jnp.float32)


def dot_nn(a, b):
    return lax.dot_general(a, b, (((1,), (0,)), ((), ())), preferred_element_type=jnp.float32)


MESH = pl.DeviceIdType.MESH


def owner_of(index, heads, seq):
    return (index * seq) // heads


def own_head(heads, seq):
    place = lax.axis_index("seq")
    index = (place * heads + seq - 1) // seq
    mine = jnp.logical_and(index < heads, owner_of(index, heads, seq) == place)
    return jnp.minimum(index, heads - 1), mine


def greet(seq, head):
    own_seq, own_group = lax.axis_index("seq"), lax.axis_index("head")
    barrier = pltpu.get_barrier_semaphore()

    def signal(i, carry):
        at = lax.rem(own_seq * head + own_group + i, seq * head)
        pl.semaphore_signal(barrier, inc=1, device_id=(at // head, lax.rem(at, head)), device_id_type=MESH)
        return carry

    lax.fori_loop(1, seq * head, signal, 0)
    pl.semaphore_wait(barrier, seq * head - 1)


def gather_kernel(seq, head, heads, *refs):
    count = 4
    ins, outs = refs[:count], refs[count : 2 * count]
    send_sem, recv_sem, own_sem = refs[2 * count :]
    own_seq, own_group = lax.axis_index("seq"), lax.axis_index("head")
    me = own_seq * head + own_group
    rows = ins[0].shape[0]
    mine_index, mine = own_head(heads, seq)
    greet(seq, head)
    total = head * heads

    def piece(group, index, array):
        column = pl.multiple_of((group * heads + index) * HD, HD)
        return ins[array].at[:, pl.ds(column, HD)]

    def place(device, array):
        return outs[array].at[pl.ds(pl.multiple_of(device * rows, rows), rows), :]

    def remote(group, index, array):
        return pltpu.make_async_remote_copy(
            src_ref=piece(group, index, array),
            dst_ref=place(me, array),
            send_sem=send_sem.at[array, group * heads + index],
            recv_sem=recv_sem.at[array, me],
            device_id=(owner_of(index, heads, seq), group),
            device_id_type=MESH,
        )

    def local(array):
        return pltpu.make_async_copy(
            piece(own_group, mine_index, array), place(me, array), own_sem.at[array]
        )

    def each_target(act):
        def step(i, carry):
            group = lax.rem(own_group + lax.rem(i, head), head)
            index = lax.rem(i // head + own_seq, heads)
            other = jnp.logical_or(group != own_group, owner_of(index, heads, seq) != own_seq)

            @pl.when(other)
            def _():
                for array in range(count):
                    act(remote(group, index, array))

            return carry

        lax.fori_loop(0, total, step, 0)

    each_target(lambda copy: copy.start())

    @pl.when(mine)
    def _():
        for array in range(count):
            local(array).start()

        def arrive(i, carry):
            source = lax.rem(me + i, seq * head)
            for array in range(count):
                pltpu.make_async_remote_copy(
                    src_ref=piece(own_group, mine_index, array),
                    dst_ref=place(source, array),
                    send_sem=send_sem.at[array, 0],
                    recv_sem=recv_sem.at[array, source],
                    device_id=(source // head, lax.rem(source, head)),
                    device_id_type=MESH,
                ).wait_recv()
            return carry

        lax.fori_loop(1, seq * head, arrive, 0)
        for array in range(count):
            local(array).wait()

    each_target(lambda copy: copy.wait_send())


def gather_heads(seq, head, heads, arrays):
    rows = arrays[0].shape[0] * seq * head
    return pl.pallas_call(
        functools.partial(gather_kernel, seq, head, heads),
        in_specs=[pl.BlockSpec(memory_space=pl.ANY)] * 4,
        out_specs=[pl.BlockSpec(memory_space=pl.ANY)] * 4,
        out_shape=[jax.ShapeDtypeStruct((rows, HD), jnp.bfloat16)] * 4,
        scratch_shapes=[
            pltpu.SemaphoreType.DMA((4, head * heads)),
            pltpu.SemaphoreType.DMA((4, seq * head)),
            pltpu.SemaphoreType.DMA((4,)),
        ],
        compiler_params=pltpu.CompilerParams(collective_id=0, has_side_effects=True),
        name="gather_heads",
    )(*arrays)


def scatter_kernel(seq, head, heads, *refs):
    video_in, text_in, video_out, text_out = refs[:4], refs[4:8], refs[8:12], refs[12:16]
    send_sem, recv_sem, own_sem, text_send, text_recv, text_own = refs[16:]
    own_seq, own_group = lax.axis_index("seq"), lax.axis_index("head")
    me = own_seq * head + own_group
    rows = video_out[0].shape[0]
    mine_index, mine = own_head(heads, seq)
    greet(seq, head)

    def part(device, array):
        return video_in[array].at[pl.ds(pl.multiple_of(device * rows, rows), rows), :]

    def column(group, index, array):
        at = pl.multiple_of((group * heads + index) * HD, HD)
        return video_out[array].at[:, pl.ds(at, HD)]

    def text_column(index, array):
        return text_out[array].at[:, pl.ds(pl.multiple_of(index * HD, HD), HD)]

    def remote(device, array):
        return pltpu.make_async_remote_copy(
            src_ref=part(device, array),
            dst_ref=column(own_group, mine_index, array),
            send_sem=send_sem.at[array, device],
            recv_sem=recv_sem.at[array, own_group * heads + mine_index],
            device_id=(device // head, lax.rem(device, head)),
            device_id_type=MESH,
        )

    def text_remote(place, array):
        return pltpu.make_async_remote_copy(
            src_ref=text_in[array],
            dst_ref=text_column(mine_index, array),
            send_sem=text_send.at[array, place],
            recv_sem=text_recv.at[array, mine_index],
            device_id=(place, own_group),
            device_id_type=MESH,
        )

    def local(array):
        return pltpu.make_async_copy(
            part(me, array), column(own_group, mine_index, array), own_sem.at[array]
        )

    def text_local(array):
        return pltpu.make_async_copy(
            text_in[array], text_column(mine_index, array), text_own.at[array]
        )

    def each(act):
        def step(i, carry):
            for array in range(4):
                act(remote(lax.rem(me + i, seq * head), array))
            return carry

        def text_step(i, carry):
            for array in range(4):
                act(text_remote(lax.rem(own_seq + i, seq), array))
            return carry

        lax.fori_loop(1, seq, text_step, 0)
        lax.fori_loop(1, seq * head, step, 0)

    @pl.when(mine)
    def _():
        each(lambda copy: copy.start())
        for array in range(4):
            local(array).start()
            text_local(array).start()

    def arrive(i, carry):
        group = i // heads
        index = lax.rem(i, heads)
        other = jnp.logical_or(group != own_group, owner_of(index, heads, seq) != own_seq)

        @pl.when(other)
        def _():
            for array in range(4):
                pltpu.make_async_remote_copy(
                    src_ref=part(0, array),
                    dst_ref=column(group, index, array),
                    send_sem=send_sem.at[array, 0],
                    recv_sem=recv_sem.at[array, group * heads + index],
                    device_id=(owner_of(index, heads, seq), group),
                    device_id_type=MESH,
                ).wait_recv()

        return carry

    def text_arrive(index, carry):
        @pl.when(owner_of(index, heads, seq) != own_seq)
        def _():
            for array in range(4):
                pltpu.make_async_remote_copy(
                    src_ref=text_in[array],
                    dst_ref=text_column(index, array),
                    send_sem=text_send.at[array, 0],
                    recv_sem=text_recv.at[array, index],
                    device_id=(owner_of(index, heads, seq), own_group),
                    device_id_type=MESH,
                ).wait_recv()

        return carry

    lax.fori_loop(0, head * heads, arrive, 0)
    lax.fori_loop(0, heads, text_arrive, 0)

    @pl.when(mine)
    def _():
        each(lambda copy: copy.wait_send())
        for array in range(4):
            local(array).wait()
            text_local(array).wait()


def scatter_heads(seq, head, heads, video, texts):
    rows = video[0].shape[0] // (seq * head)
    text = texts[0].shape[0]
    return pl.pallas_call(
        functools.partial(scatter_kernel, seq, head, heads),
        in_specs=[pl.BlockSpec(memory_space=pl.ANY)] * 8,
        out_specs=[pl.BlockSpec(memory_space=pl.ANY)] * 8,
        out_shape=[jax.ShapeDtypeStruct((rows, head * heads * HD), jnp.bfloat16)] * 4
        + [jax.ShapeDtypeStruct((text, heads * HD), jnp.bfloat16)] * 4,
        scratch_shapes=[
            pltpu.SemaphoreType.DMA((4, seq * head)),
            pltpu.SemaphoreType.DMA((4, head * heads)),
            pltpu.SemaphoreType.DMA((4,)),
            pltpu.SemaphoreType.DMA((4, seq)),
            pltpu.SemaphoreType.DMA((4, heads)),
            pltpu.SemaphoreType.DMA((4,)),
        ],
        compiler_params=pltpu.CompilerParams(collective_id=1, has_side_effects=True),
        name="scatter_heads",
    )(*video, *texts)


def text_pass(refs):
    (k_ref, v_ref, tq_ref, tg_ref, tk_ref, tv_ref, bias_ref, to_ref, tdq_ref, sbuf, dk_acc, dv_acc) = refs
    video = k_ref.shape[0]
    text = tk_ref.shape[0]
    scale2 = FACTOR * LOG2E
    block = 512
    steps = video // block
    tq = tq_ref[...]
    tg = tg_ref[...]
    text_s = dot_nt(tk_ref[...], tq) * scale2 + bias_ref[:, :1]
    top = jnp.max(text_s, axis=0, keepdims=True)

    def scores(i, top):
        rows = pl.ds(pl.multiple_of(i * block, block), block)
        s = dot_nt(k_ref[rows, :], tq) * scale2
        sbuf[rows, :] = s
        return jnp.maximum(top, jnp.max(s, axis=0, keepdims=True))

    top = lax.fori_loop(0, steps, scores, top)
    text_e = jnp.exp2(text_s - top)

    def weigh(i, carry):
        total, out = carry
        rows = pl.ds(pl.multiple_of(i * block, block), block)
        e = jnp.exp2(sbuf[rows, :] - top)
        sbuf[rows, :] = e
        out = out + dot_tn(e.astype(jnp.bfloat16), v_ref[rows, :])
        return total + jnp.sum(e, axis=0, keepdims=True), out

    total, out = lax.fori_loop(
        0,
        steps,
        weigh,
        (
            jnp.sum(text_e, axis=0, keepdims=True),
            dot_tn(text_e.astype(jnp.bfloat16), tv_ref[...]),
        ),
    )
    inverse = 1.0 / total
    out = out * jnp.transpose(inverse)
    to_ref[...] = out.astype(jnp.bfloat16)
    delta = jnp.transpose(jnp.sum(tg.astype(jnp.float32) * out, axis=1, keepdims=True))

    def spread(e, key, value):
        p = e * inverse
        dv = dot_nn(p.astype(jnp.bfloat16), tg)
        ds = (p * (dot_nt(value, tg) - delta)).astype(jnp.bfloat16)
        return dot_nn(ds, tq), dv, dot_tn(ds, key)

    dk, dv, dq = spread(text_e, tk_ref[...], tv_ref[...])
    dk_acc[pl.ds(video, text), :] = dk
    dv_acc[pl.ds(video, text), :] = dv

    def back(i, dq):
        rows = pl.ds(pl.multiple_of(i * block, block), block)
        dk, dv, more = spread(sbuf[rows, :], k_ref[rows, :], v_ref[rows, :])
        dk_acc[rows, :] = dk
        dv_acc[rows, :] = dv
        return dq + more

    dq = lax.fori_loop(0, steps, back, dq)
    tdq_ref[...] = (dq * FACTOR).astype(jnp.bfloat16)


def attend_kernel(
    entries,
    own_ref,
    slot_ref,
    count_ref,
    q_ref,
    g_ref,
    k_ref,
    v_ref,
    tq_ref,
    tg_ref,
    tk_ref,
    tv_ref,
    bias_ref,
    o_ref,
    dq_ref,
    dk_ref,
    dv_ref,
    to_ref,
    tdq_ref,
    tdk_ref,
    tdv_ref,
    kbuf,
    vbuf,
    sbuf,
    dk_acc,
    dv_acc,
):
    video = k_ref.shape[0]
    text = tk_ref.shape[0]
    chunk = q_ref.shape[0]
    listed = entries * TILE
    scale2 = FACTOR * LOG2E
    step = pl.program_id(0)
    active = own_ref[1] > 0

    @pl.when(jnp.logical_and(active, step == 0))
    def _():
        kbuf[pl.ds(listed, text), :] = tk_ref[...]
        vbuf[pl.ds(listed, text), :] = tv_ref[...]
        text_pass(
            (k_ref, v_ref, tq_ref, tg_ref, tk_ref, tv_ref, bias_ref, to_ref, tdq_ref, sbuf, dk_acc, dv_acc)
        )

    def tile(i, carry):
        rows = pl.ds(pl.multiple_of(i * TILE, TILE), TILE)
        number = step * (chunk // TILE) + i
        spots = [
            pl.ds(pl.multiple_of(slot_ref[number * entries + e] * TILE, TILE), TILE)
            for e in range(entries)
        ]
        count = count_ref[number]
        q = q_ref[rows, :]
        g = g_ref[rows, :]
        for e in range(entries):
            kbuf[pl.ds(e * TILE, TILE), :] = k_ref[spots[e], :]
            vbuf[pl.ds(e * TILE, TILE), :] = v_ref[spots[e], :]
        keys = kbuf[...]
        values = vbuf[...]
        s = dot_nt(keys, q) * scale2
        parts = [
            s[e * TILE : (e + 1) * TILE] + jnp.where(e < count, 0.0, NEGATIVE)
            for e in range(entries)
        ]
        s = jnp.concatenate(parts + [s[listed:] + bias_ref[...]], axis=0)
        e = jnp.exp2(s - jnp.max(s, axis=0, keepdims=True))
        p = e * (1.0 / jnp.sum(e, axis=0, keepdims=True))
        weights = p.astype(jnp.bfloat16)
        out = dot_tn(weights, values)
        o_ref[rows, :] = out.astype(jnp.bfloat16)
        delta = jnp.transpose(jnp.sum(g.astype(jnp.float32) * out, axis=1, keepdims=True))
        ds = (p * (dot_nt(values, g) - delta)).astype(jnp.bfloat16)
        dq_ref[rows, :] = (dot_tn(ds, keys) * FACTOR).astype(jnp.bfloat16)
        dk = dot_nn(ds, q)
        dv = dot_nn(weights, g)
        for e in range(entries):
            dk_acc[spots[e], :] += dk[e * TILE : (e + 1) * TILE]
            dv_acc[spots[e], :] += dv[e * TILE : (e + 1) * TILE]
        dk_acc[pl.ds(video, text), :] += dk[listed:]
        dv_acc[pl.ds(video, text), :] += dv[listed:]
        return carry

    @pl.when(active)
    def _():
        lax.fori_loop(0, chunk // TILE, tile, 0)

    @pl.when(jnp.logical_and(active, step == pl.num_programs(0) - 1))
    def _():
        dk_ref[...] = (dk_acc[pl.ds(0, video), :] * FACTOR).astype(dk_ref.dtype)
        dv_ref[...] = dv_acc[pl.ds(0, video), :].astype(dv_ref.dtype)
        tdk_ref[...] = (dk_acc[pl.ds(video, text), :] * FACTOR).astype(tdk_ref.dtype)
        tdv_ref[...] = dv_acc[pl.ds(video, text), :].astype(tdv_ref.dtype)


def attend(own, slots, counts, q, g, k, v, tq, tg, tk, tv, bias):
    video = k.shape[0]
    text = tk.shape[0]
    entries = slots.shape[1]
    chunk = min(video, 1024)
    total = video + text
    block = pl.BlockSpec((chunk, HD), lambda i, *_: (i, 0))
    held = pl.BlockSpec((video, HD), lambda i, *_: (0, 0), pipeline_mode=pl.Buffered(1))
    given = pl.BlockSpec((text, HD), lambda i, own, *_: (0, own[0]))
    made = pl.BlockSpec((text, HD), lambda i, *_: (0, 0))
    whole = pl.BlockSpec((video, HD), lambda i, *_: (0, 0))
    video_shape = jax.ShapeDtypeStruct((video, HD), jnp.bfloat16)
    text_shape = jax.ShapeDtypeStruct((text, HD), jnp.bfloat16)
    call = pl.pallas_call(
        functools.partial(attend_kernel, entries),
        grid_spec=pltpu.PrefetchScalarGridSpec(
            num_scalar_prefetch=3,
            grid=(video // chunk,),
            in_specs=[block, block, held, held, given, given, given, given, made],
            out_specs=[block, block, whole, whole, made, made, made, made],
            scratch_shapes=[
                pltpu.VMEM((entries * TILE + text, HD), jnp.bfloat16),
                pltpu.VMEM((entries * TILE + text, HD), jnp.bfloat16),
                pltpu.VMEM((video, text), jnp.float32),
                pltpu.VMEM((total, HD), jnp.float32),
                pltpu.VMEM((total, HD), jnp.float32),
            ],
        ),
        out_shape=[video_shape] * 4 + [text_shape] * 4,
        compiler_params=pltpu.CompilerParams(vmem_limit_bytes=63 * 1024 * 1024),
        name="attend",
    )
    return call(own, slots.reshape(-1), counts, q, g, k, v, tq, tg, tk, tv, bias)


def body(
    video_query,
    video_key,
    video_value,
    video_grad,
    text_query,
    text_key,
    text_value,
    text_grad,
    tile_list,
    tile_count,
    text_mask,
):
    seq, head = lax.axis_size("seq"), lax.axis_size("head")
    text, width = text_query.shape
    heads = width // HD
    keys, values, queries, grads = gather_heads(
        seq, head, heads, (video_key, video_value, video_query, video_grad)
    )
    index, mine = own_head(heads, seq)
    own = jnp.stack([index, mine.astype(jnp.int32)]).astype(jnp.int32)
    bias = jnp.broadcast_to(
        jnp.where(text_mask > 0, 0.0, NEGATIVE).astype(jnp.float32)[:, None], (text, HD)
    )
    o, dq, dk, dv, to, tdq, tdk, tdv = attend(
        own,
        tile_list,
        tile_count,
        queries,
        grads,
        keys,
        values,
        text_query,
        text_grad,
        text_key,
        text_value,
        bias,
    )
    return tuple(scatter_heads(seq, head, heads, (o, dq, dk, dv), (to, tdq, tdk, tdv)))


def solution(mesh):
    video = P(("seq", "head"), None)
    side = P(None, "head")
    return jax.shard_map(
        body,
        mesh=mesh,
        in_specs=(video,) * 4 + (side,) * 4 + (P(), P(), P()),
        out_specs=(video,) * 4 + (side,) * 4,
        check_vma=False,
    )
```

```python
import functools

import jax
import jax.numpy as jnp
from jax import lax
from jax.experimental import pallas as pl
from jax.experimental.pallas import tpu as pltpu
from jax.sharding import PartitionSpec as P

HD = 128
TILE = 128
NEGATIVE = -1e30
LOG2E = 1.4426950408889634
FACTOR = HD**-0.5


def dot_nt(a, b):
    return lax.dot_general(a, b, (((1,), (1,)), ((), ())), preferred_element_type=jnp.float32)


def dot_tn(a, b):
    return lax.dot_general(a, b, (((0,), (0,)), ((), ())), preferred_element_type=jnp.float32)


def dot_nn(a, b):
    return lax.dot_general(a, b, (((1,), (0,)), ((), ())), preferred_element_type=jnp.float32)


MESH = pl.DeviceIdType.MESH


def owner_of(index, heads, seq):
    return (index * seq) // heads


def own_head(heads, seq):
    place = lax.axis_index("seq")
    index = (place * heads + seq - 1) // seq
    mine = jnp.logical_and(index < heads, owner_of(index, heads, seq) == place)
    return jnp.minimum(index, heads - 1), mine


def greet(seq, head):
    own_seq, own_group = lax.axis_index("seq"), lax.axis_index("head")
    barrier = pltpu.get_barrier_semaphore()

    def signal(i, carry):
        at = lax.rem(own_seq * head + own_group + i, seq * head)
        pl.semaphore_signal(barrier, inc=1, device_id=(at // head, lax.rem(at, head)), device_id_type=MESH)
        return carry

    lax.fori_loop(1, seq * head, signal, 0)
    pl.semaphore_wait(barrier, seq * head - 1)


def gather_kernel(seq, head, heads, *refs):
    count = 4
    ins, outs = refs[:count], refs[count : 2 * count]
    send_sem, recv_sem, own_sem = refs[2 * count :]
    own_seq, own_group = lax.axis_index("seq"), lax.axis_index("head")
    me = own_seq * head + own_group
    rows = ins[0].shape[0]
    mine_index, mine = own_head(heads, seq)
    greet(seq, head)
    total = head * heads

    def piece(group, index, array):
        column = pl.multiple_of((group * heads + index) * HD, HD)
        return ins[array].at[:, pl.ds(column, HD)]

    def place(device, array):
        return outs[array].at[pl.ds(pl.multiple_of(device * rows, rows), rows), :]

    def remote(group, index, array):
        return pltpu.make_async_remote_copy(
            src_ref=piece(group, index, array),
            dst_ref=place(me, array),
            send_sem=send_sem.at[array, group * heads + index],
            recv_sem=recv_sem.at[array, me],
            device_id=(owner_of(index, heads, seq), group),
            device_id_type=MESH,
        )

    def local(array):
        return pltpu.make_async_copy(
            piece(own_group, mine_index, array), place(me, array), own_sem.at[array]
        )

    def each_target(act):
        def step(i, carry):
            group = lax.rem(own_group + lax.rem(i, head), head)
            index = lax.rem(i // head + own_seq, heads)
            other = jnp.logical_or(group != own_group, owner_of(index, heads, seq) != own_seq)

            @pl.when(other)
            def _():
                for array in range(count):
                    act(remote(group, index, array))

            return carry

        lax.fori_loop(0, total, step, 0)

    each_target(lambda copy: copy.start())

    @pl.when(mine)
    def _():
        for array in range(count):
            local(array).start()

        def arrive(i, carry):
            source = lax.rem(me + i, seq * head)
            for array in range(count):
                pltpu.make_async_remote_copy(
                    src_ref=piece(own_group, mine_index, array),
                    dst_ref=place(source, array),
                    send_sem=send_sem.at[array, 0],
                    recv_sem=recv_sem.at[array, source],
                    device_id=(source // head, lax.rem(source, head)),
                    device_id_type=MESH,
                ).wait_recv()
            return carry

        lax.fori_loop(1, seq * head, arrive, 0)
        for array in range(count):
            local(array).wait()

    each_target(lambda copy: copy.wait_send())


def gather_heads(seq, head, heads, arrays):
    rows = arrays[0].shape[0] * seq * head
    return pl.pallas_call(
        functools.partial(gather_kernel, seq, head, heads),
        in_specs=[pl.BlockSpec(memory_space=pl.ANY)] * 4,
        out_specs=[pl.BlockSpec(memory_space=pl.ANY)] * 4,
        out_shape=[jax.ShapeDtypeStruct((rows, HD), jnp.bfloat16)] * 4,
        scratch_shapes=[
            pltpu.SemaphoreType.DMA((4, head * heads)),
            pltpu.SemaphoreType.DMA((4, seq * head)),
            pltpu.SemaphoreType.DMA((4,)),
        ],
        compiler_params=pltpu.CompilerParams(collective_id=0, has_side_effects=True),
        name="gather_heads",
    )(*arrays)


def scatter_kernel(seq, head, heads, *refs):
    video_in, text_in, video_out, text_out = refs[:4], refs[4:8], refs[8:12], refs[12:16]
    send_sem, recv_sem, own_sem, text_send, text_recv, text_own = refs[16:]
    own_seq, own_group = lax.axis_index("seq"), lax.axis_index("head")
    me = own_seq * head + own_group
    rows = video_out[0].shape[0]
    mine_index, mine = own_head(heads, seq)
    cores = 2 if seq % 2 == 0 else 1
    greet(seq, head)

    def part(device, array):
        return video_in[array].at[pl.ds(pl.multiple_of(device * rows, rows), rows), :]

    def column(group, index, array):
        at = pl.multiple_of((group * heads + index) * HD, HD)
        return video_out[array].at[:, pl.ds(at, HD)]

    def text_column(index, array):
        return text_out[array].at[:, pl.ds(pl.multiple_of(index * HD, HD), HD)]

    def remote(device, array):
        return pltpu.make_async_remote_copy(
            src_ref=part(device, array),
            dst_ref=column(own_group, mine_index, array),
            send_sem=send_sem.at[array, device],
            recv_sem=recv_sem.at[array, own_group * heads + mine_index],
            device_id=(device // head, lax.rem(device, head)),
            device_id_type=MESH,
        )

    def text_remote(source, index, array, way, place):
        return pltpu.make_async_remote_copy(
            src_ref=source,
            dst_ref=text_column(index, array),
            send_sem=text_send.at[array, index, way],
            recv_sem=text_recv.at[array, index],
            device_id=(place, own_group),
            device_id_type=MESH,
        )

    def text_sends(act, index, sources):
        chip, chips = own_seq // cores, seq // cores
        home = owner_of(index, heads, seq) // cores
        for way, shift in enumerate((1, -1)):
            far = chip + shift
            inside = jnp.logical_and(far >= 0, far < chips)

            @pl.when(jnp.logical_and(inside, (chip - home) * shift >= 0))
            def _():
                for array in range(4):
                    act(text_remote(sources(array), index, array, way, far * cores + own_seq % cores))

        if cores == 2:
            for array in range(4):
                act(text_remote(sources(array), index, array, 2, chip * cores + 1 - own_seq % cores))

    def local(array):
        return pltpu.make_async_copy(
            part(me, array), column(own_group, mine_index, array), own_sem.at[array]
        )

    def text_local(array):
        return pltpu.make_async_copy(
            text_in[array], text_column(mine_index, array), text_own.at[array]
        )

    def each(act):
        def step(i, carry):
            for array in range(4):
                act(remote(lax.rem(me + i, seq * head), array))
            return carry

        text_sends(act, mine_index, lambda array: text_in[array])
        lax.fori_loop(1, seq * head, step, 0)

    @pl.when(mine)
    def _():
        each(lambda copy: copy.start())
        for array in range(4):
            local(array).start()
            text_local(array).start()

    def arrive(i, carry):
        group = i // heads
        index = lax.rem(i, heads)
        other = jnp.logical_or(group != own_group, owner_of(index, heads, seq) != own_seq)

        @pl.when(other)
        def _():
            for array in range(4):
                pltpu.make_async_remote_copy(
                    src_ref=part(0, array),
                    dst_ref=column(group, index, array),
                    send_sem=send_sem.at[array, 0],
                    recv_sem=recv_sem.at[array, group * heads + index],
                    device_id=(owner_of(index, heads, seq), group),
                    device_id_type=MESH,
                ).wait_recv()

        return carry

    def text_arrive(index, carry):
        @pl.when(owner_of(index, heads, seq) != own_seq)
        def _():
            for array in range(4):
                text_remote(text_in[array], index, array, 0, owner_of(index, heads, seq)).wait_recv()
            pl.when(relays(index))(
                lambda: text_sends(
                    lambda copy: copy.start(), index, lambda array: text_column(index, array)
                )
            )

        return carry

    def relays(index):
        owner = owner_of(index, heads, seq)
        return jnp.logical_and(owner != own_seq, owner % cores == own_seq % cores)

    def text_relayed(index, carry):
        pl.when(relays(index))(
            lambda: text_sends(
                lambda copy: copy.wait_send(), index, lambda array: text_column(index, array)
            )
        )
        return carry

    lax.fori_loop(0, heads, text_arrive, 0)
    lax.fori_loop(0, head * heads, arrive, 0)
    lax.fori_loop(0, heads, text_relayed, 0)

    @pl.when(mine)
    def _():
        each(lambda copy: copy.wait_send())
        for array in range(4):
            local(array).wait()
            text_local(array).wait()


def scatter_heads(seq, head, heads, video, texts):
    rows = video[0].shape[0] // (seq * head)
    text = texts[0].shape[0]
    return pl.pallas_call(
        functools.partial(scatter_kernel, seq, head, heads),
        in_specs=[pl.BlockSpec(memory_space=pl.ANY)] * 8,
        out_specs=[pl.BlockSpec(memory_space=pl.ANY)] * 8,
        out_shape=[jax.ShapeDtypeStruct((rows, head * heads * HD), jnp.bfloat16)] * 4
        + [jax.ShapeDtypeStruct((text, heads * HD), jnp.bfloat16)] * 4,
        scratch_shapes=[
            pltpu.SemaphoreType.DMA((4, seq * head)),
            pltpu.SemaphoreType.DMA((4, head * heads)),
            pltpu.SemaphoreType.DMA((4,)),
            pltpu.SemaphoreType.DMA((4, heads, 3)),
            pltpu.SemaphoreType.DMA((4, heads)),
            pltpu.SemaphoreType.DMA((4,)),
        ],
        compiler_params=pltpu.CompilerParams(collective_id=1, has_side_effects=True),
        name="scatter_heads",
    )(*video, *texts)


def text_pass(refs):
    (k_ref, v_ref, tq_ref, tg_ref, tk_ref, tv_ref, bias_ref, to_ref, tdq_ref, sbuf, dk_acc, dv_acc) = refs
    video = k_ref.shape[0]
    text = tk_ref.shape[0]
    scale2 = FACTOR * LOG2E
    block = 512
    steps = video // block
    tq = tq_ref[...]
    tg = tg_ref[...]
    text_s = dot_nt(tk_ref[...], tq) * scale2 + bias_ref[:, :1]
    top = jnp.max(text_s, axis=0, keepdims=True)

    def scores(i, top):
        rows = pl.ds(pl.multiple_of(i * block, block), block)
        s = dot_nt(k_ref[rows, :], tq) * scale2
        sbuf[rows, :] = s
        return jnp.maximum(top, jnp.max(s, axis=0, keepdims=True))

    top = lax.fori_loop(0, steps, scores, top)
    text_e = jnp.exp2(text_s - top)

    def weigh(i, carry):
        total, out = carry
        rows = pl.ds(pl.multiple_of(i * block, block), block)
        e = jnp.exp2(sbuf[rows, :] - top)
        sbuf[rows, :] = e
        out = out + dot_tn(e.astype(jnp.bfloat16), v_ref[rows, :])
        return total + jnp.sum(e, axis=0, keepdims=True), out

    total, out = lax.fori_loop(
        0,
        steps,
        weigh,
        (
            jnp.sum(text_e, axis=0, keepdims=True),
            dot_tn(text_e.astype(jnp.bfloat16), tv_ref[...]),
        ),
    )
    inverse = 1.0 / total
    out = out * jnp.transpose(inverse)
    to_ref[...] = out.astype(jnp.bfloat16)
    delta = jnp.transpose(jnp.sum(tg.astype(jnp.float32) * out, axis=1, keepdims=True))

    def spread(e, key, value):
        p = e * inverse
        dv = dot_nn(p.astype(jnp.bfloat16), tg)
        ds = (p * (dot_nt(value, tg) - delta)).astype(jnp.bfloat16)
        return dot_nn(ds, tq), dv, dot_tn(ds, key)

    dk, dv, dq = spread(text_e, tk_ref[...], tv_ref[...])
    dk_acc[pl.ds(video, text), :] = dk
    dv_acc[pl.ds(video, text), :] = dv

    def back(i, dq):
        rows = pl.ds(pl.multiple_of(i * block, block), block)
        dk, dv, more = spread(sbuf[rows, :], k_ref[rows, :], v_ref[rows, :])
        dk_acc[rows, :] = dk
        dv_acc[rows, :] = dv
        return dq + more

    dq = lax.fori_loop(0, steps, back, dq)
    tdq_ref[...] = (dq * FACTOR).astype(jnp.bfloat16)


def attend_kernel(
    entries,
    own_ref,
    slot_ref,
    count_ref,
    q_ref,
    g_ref,
    k_ref,
    v_ref,
    tq_ref,
    tg_ref,
    tk_ref,
    tv_ref,
    bias_ref,
    o_ref,
    dq_ref,
    dk_ref,
    dv_ref,
    to_ref,
    tdq_ref,
    tdk_ref,
    tdv_ref,
    kbuf,
    vbuf,
    sbuf,
    dk_acc,
    dv_acc,
):
    video = k_ref.shape[0]
    text = tk_ref.shape[0]
    chunk = q_ref.shape[0]
    scale2 = FACTOR * LOG2E
    step = pl.program_id(0)
    active = own_ref[1] > 0

    @pl.when(jnp.logical_and(active, step == 0))
    def _():
        kbuf[pl.ds(0, text), :] = tk_ref[...]
        vbuf[pl.ds(0, text), :] = tv_ref[...]
        text_pass(
            (k_ref, v_ref, tq_ref, tg_ref, tk_ref, tv_ref, bias_ref, to_ref, tdq_ref, sbuf, dk_acc, dv_acc)
        )

    def tile_of(i, used):
        rows = pl.ds(pl.multiple_of(i * TILE, TILE), TILE)
        number = step * (chunk // TILE) + i
        spots = [
            pl.ds(pl.multiple_of(slot_ref[number * entries + e] * TILE, TILE), TILE)
            for e in range(used)
        ]
        q = q_ref[rows, :]
        g = g_ref[rows, :]
        for e in range(used):
            kbuf[pl.ds(text + e * TILE, TILE), :] = k_ref[spots[e], :]
            vbuf[pl.ds(text + e * TILE, TILE), :] = v_ref[spots[e], :]
        keys = kbuf[pl.ds(0, text + used * TILE), :]
        values = vbuf[pl.ds(0, text + used * TILE), :]
        s = dot_nt(keys, q) * scale2
        s = jnp.concatenate([s[:text] + bias_ref[...], s[text:]], axis=0)
        e = jnp.exp2(s - jnp.max(s, axis=0, keepdims=True))
        p = e * (1.0 / jnp.sum(e, axis=0, keepdims=True))
        weights = p.astype(jnp.bfloat16)
        out = dot_tn(weights, values)
        o_ref[rows, :] = out.astype(jnp.bfloat16)
        delta = jnp.transpose(jnp.sum(g.astype(jnp.float32) * out, axis=1, keepdims=True))
        ds = (p * (dot_nt(values, g) - delta)).astype(jnp.bfloat16)
        dq_ref[rows, :] = (dot_tn(ds, keys) * FACTOR).astype(jnp.bfloat16)
        dk = dot_nn(ds, q)
        dv = dot_nn(weights, g)
        for e in range(used):
            at = text + e * TILE
            dk_acc[spots[e], :] += dk[at : at + TILE]
            dv_acc[spots[e], :] += dv[at : at + TILE]
        dk_acc[pl.ds(video, text), :] += dk[:text]
        dv_acc[pl.ds(video, text), :] += dv[:text]

    def tile(i, carry):
        count = count_ref[step * (chunk // TILE) + i]
        for used in range(1, entries + 1):
            pl.when(count == used)(functools.partial(tile_of, i, used))
        return carry

    @pl.when(active)
    def _():
        lax.fori_loop(0, chunk // TILE, tile, 0)

    @pl.when(jnp.logical_and(active, step == pl.num_programs(0) - 1))
    def _():
        dk_ref[...] = (dk_acc[pl.ds(0, video), :] * FACTOR).astype(dk_ref.dtype)
        dv_ref[...] = dv_acc[pl.ds(0, video), :].astype(dv_ref.dtype)
        tdk_ref[...] = (dk_acc[pl.ds(video, text), :] * FACTOR).astype(tdk_ref.dtype)
        tdv_ref[...] = dv_acc[pl.ds(video, text), :].astype(tdv_ref.dtype)


def attend(own, slots, counts, q, g, k, v, tq, tg, tk, tv, bias):
    video = k.shape[0]
    text = tk.shape[0]
    entries = slots.shape[1]
    chunk = min(video, 1024)
    total = video + text
    block = pl.BlockSpec((chunk, HD), lambda i, *_: (i, 0))
    held = pl.BlockSpec((video, HD), lambda i, *_: (0, 0), pipeline_mode=pl.Buffered(1))
    given = pl.BlockSpec((text, HD), lambda i, own, *_: (0, own[0]))
    made = pl.BlockSpec((text, HD), lambda i, *_: (0, 0))
    whole = pl.BlockSpec((video, HD), lambda i, *_: (0, 0))
    video_shape = jax.ShapeDtypeStruct((video, HD), jnp.bfloat16)
    text_shape = jax.ShapeDtypeStruct((text, HD), jnp.bfloat16)
    call = pl.pallas_call(
        functools.partial(attend_kernel, entries),
        grid_spec=pltpu.PrefetchScalarGridSpec(
            num_scalar_prefetch=3,
            grid=(video // chunk,),
            in_specs=[block, block, held, held, given, given, given, given, made],
            out_specs=[block, block, whole, whole, made, made, made, made],
            scratch_shapes=[
                pltpu.VMEM((entries * TILE + text, HD), jnp.bfloat16),
                pltpu.VMEM((entries * TILE + text, HD), jnp.bfloat16),
                pltpu.VMEM((video, text), jnp.float32),
                pltpu.VMEM((total, HD), jnp.float32),
                pltpu.VMEM((total, HD), jnp.float32),
            ],
        ),
        out_shape=[video_shape] * 4 + [text_shape] * 4,
        compiler_params=pltpu.CompilerParams(vmem_limit_bytes=63 * 1024 * 1024),
        name="attend",
    )
    return call(own, slots.reshape(-1), counts, q, g, k, v, tq, tg, tk, tv, bias)


def body(
    video_query,
    video_key,
    video_value,
    video_grad,
    text_query,
    text_key,
    text_value,
    text_grad,
    tile_list,
    tile_count,
    text_mask,
):
    seq, head = lax.axis_size("seq"), lax.axis_size("head")
    text, width = text_query.shape
    heads = width // HD
    keys, values, queries, grads = gather_heads(
        seq, head, heads, (video_key, video_value, video_query, video_grad)
    )
    index, mine = own_head(heads, seq)
    own = jnp.stack([index, mine.astype(jnp.int32)]).astype(jnp.int32)
    bias = jnp.broadcast_to(
        jnp.where(text_mask > 0, 0.0, NEGATIVE).astype(jnp.float32)[:, None], (text, HD)
    )
    o, dq, dk, dv, to, tdq, tdk, tdv = attend(
        own,
        tile_list,
        tile_count,
        queries,
        grads,
        keys,
        values,
        text_query,
        text_grad,
        text_key,
        text_value,
        bias,
    )
    return tuple(scatter_heads(seq, head, heads, (o, dq, dk, dv), (to, tdq, tdk, tdv)))


def solution(mesh):
    video = P(("seq", "head"), None)
    side = P(None, "head")
    return jax.shard_map(
        body,
        mesh=mesh,
        in_specs=(video,) * 4 + (side,) * 4 + (P(), P(), P()),
        out_specs=(video,) * 4 + (side,) * 4,
        check_vma=False,
    )
```

```python
import functools

import jax
import jax.numpy as jnp
from jax import lax
from jax.experimental import pallas as pl
from jax.experimental.pallas import tpu as pltpu
from jax.sharding import PartitionSpec as P

HD = 128
TILE = 128
NEGATIVE = -1e30
LOG2E = 1.4426950408889634
FACTOR = HD**-0.5


def dot_nt(a, b):
    return lax.dot_general(a, b, (((1,), (1,)), ((), ())), preferred_element_type=jnp.float32)


def dot_tn(a, b):
    return lax.dot_general(a, b, (((0,), (0,)), ((), ())), preferred_element_type=jnp.float32)


def dot_nn(a, b):
    return lax.dot_general(a, b, (((1,), (0,)), ((), ())), preferred_element_type=jnp.float32)


MESH = pl.DeviceIdType.MESH


def owner_of(index, heads, seq):
    return (index * seq) // heads


def own_head(heads, seq):
    place = lax.axis_index("seq")
    index = (place * heads + seq - 1) // seq
    mine = jnp.logical_and(index < heads, owner_of(index, heads, seq) == place)
    return jnp.minimum(index, heads - 1), mine


def greet(seq, head):
    own_seq, own_group = lax.axis_index("seq"), lax.axis_index("head")
    barrier = pltpu.get_barrier_semaphore()

    def signal(i, carry):
        at = lax.rem(own_seq * head + own_group + i, seq * head)
        pl.semaphore_signal(barrier, inc=1, device_id=(at // head, lax.rem(at, head)), device_id_type=MESH)
        return carry

    lax.fori_loop(1, seq * head, signal, 0)
    pl.semaphore_wait(barrier, seq * head - 1)


def gather_kernel(seq, head, heads, *refs):
    count = 4
    ins, outs = refs[:count], refs[count : 2 * count]
    send_sem, recv_sem, own_sem = refs[2 * count :]
    own_seq, own_group = lax.axis_index("seq"), lax.axis_index("head")
    me = own_seq * head + own_group
    rows = ins[0].shape[0]
    mine_index, mine = own_head(heads, seq)
    greet(seq, head)
    total = head * heads

    def piece(group, index, array):
        column = pl.multiple_of((group * heads + index) * HD, HD)
        return ins[array].at[:, pl.ds(column, HD)]

    def place(device, array):
        return outs[array].at[pl.ds(pl.multiple_of(device * rows, rows), rows), :]

    def remote(group, index, array):
        return pltpu.make_async_remote_copy(
            src_ref=piece(group, index, array),
            dst_ref=place(me, array),
            send_sem=send_sem.at[array, group * heads + index],
            recv_sem=recv_sem.at[array, me],
            device_id=(owner_of(index, heads, seq), group),
            device_id_type=MESH,
        )

    def local(array):
        return pltpu.make_async_copy(
            piece(own_group, mine_index, array), place(me, array), own_sem.at[array]
        )

    def each_target(act):
        def step(i, carry):
            group = lax.rem(own_group + lax.rem(i, head), head)
            index = lax.rem(i // head + own_seq, heads)
            other = jnp.logical_or(group != own_group, owner_of(index, heads, seq) != own_seq)

            @pl.when(other)
            def _():
                for array in range(count):
                    act(remote(group, index, array))

            return carry

        lax.fori_loop(0, total, step, 0)

    each_target(lambda copy: copy.start())

    @pl.when(mine)
    def _():
        for array in range(count):
            local(array).start()

        def arrive(i, carry):
            source = lax.rem(me + i, seq * head)
            for array in range(count):
                pltpu.make_async_remote_copy(
                    src_ref=piece(own_group, mine_index, array),
                    dst_ref=place(source, array),
                    send_sem=send_sem.at[array, 0],
                    recv_sem=recv_sem.at[array, source],
                    device_id=(source // head, lax.rem(source, head)),
                    device_id_type=MESH,
                ).wait_recv()
            return carry

        lax.fori_loop(1, seq * head, arrive, 0)
        for array in range(count):
            local(array).wait()

    each_target(lambda copy: copy.wait_send())


def gather_heads(seq, head, heads, arrays):
    rows = arrays[0].shape[0] * seq * head
    return pl.pallas_call(
        functools.partial(gather_kernel, seq, head, heads),
        in_specs=[pl.BlockSpec(memory_space=pl.ANY)] * 4,
        out_specs=[pl.BlockSpec(memory_space=pl.ANY)] * 4,
        out_shape=[jax.ShapeDtypeStruct((rows, HD), jnp.bfloat16)] * 4,
        scratch_shapes=[
            pltpu.SemaphoreType.DMA((4, head * heads)),
            pltpu.SemaphoreType.DMA((4, seq * head)),
            pltpu.SemaphoreType.DMA((4,)),
        ],
        compiler_params=pltpu.CompilerParams(collective_id=0, has_side_effects=True),
        name="gather_heads",
    )(*arrays)


def scatter_kernel(seq, head, heads, *refs):
    video_in, text_in, video_out, text_out = refs[:4], refs[4:8], refs[8:12], refs[12:16]
    send_sem, recv_sem, own_sem, text_send, text_recv, text_own = refs[16:]
    own_seq, own_group = lax.axis_index("seq"), lax.axis_index("head")
    me = own_seq * head + own_group
    rows = video_out[0].shape[0]
    mine_index, mine = own_head(heads, seq)
    cores = 2 if seq % 2 == 0 else 1
    greet(seq, head)

    def part(device, array):
        return video_in[array].at[pl.ds(pl.multiple_of(device * rows, rows), rows), :]

    def column(group, index, array):
        at = pl.multiple_of((group * heads + index) * HD, HD)
        return video_out[array].at[:, pl.ds(at, HD)]

    def text_column(index, array):
        return text_out[array].at[:, pl.ds(pl.multiple_of(index * HD, HD), HD)]

    def remote(device, array):
        return pltpu.make_async_remote_copy(
            src_ref=part(device, array),
            dst_ref=column(own_group, mine_index, array),
            send_sem=send_sem.at[array, device],
            recv_sem=recv_sem.at[array, own_group * heads + mine_index],
            device_id=(device // head, lax.rem(device, head)),
            device_id_type=MESH,
        )

    def text_remote(source, index, array, place):
        return pltpu.make_async_remote_copy(
            src_ref=source,
            dst_ref=text_column(index, array),
            send_sem=text_send.at[array, index, place],
            recv_sem=text_recv.at[array, index],
            device_id=(place, own_group),
            device_id_type=MESH,
        )

    def text_beside(act, index, sources):
        if cores == 2:
            for array in range(4):
                act(text_remote(sources(array), index, array, own_seq + 1 - 2 * (own_seq % 2)))

    def text_far(act, index, sources):
        def step(i, carry):
            for array in range(4):
                act(text_remote(sources(array), index, array, lax.rem(own_seq + i * cores, seq)))
            return carry

        lax.fori_loop(1, seq // cores, step, 0)

    def local(array):
        return pltpu.make_async_copy(
            part(me, array), column(own_group, mine_index, array), own_sem.at[array]
        )

    def text_local(array):
        return pltpu.make_async_copy(
            text_in[array], text_column(mine_index, array), text_own.at[array]
        )

    def each(act):
        def step(i, carry):
            for array in range(4):
                act(remote(lax.rem(me + i, seq * head), array))
            return carry

        text_far(act, mine_index, lambda array: text_in[array])
        text_beside(act, mine_index, lambda array: text_in[array])
        lax.fori_loop(1, seq * head, step, 0)

    @pl.when(mine)
    def _():
        each(lambda copy: copy.start())
        for array in range(4):
            local(array).start()
            text_local(array).start()

    def arrive(i, carry):
        group = i // heads
        index = lax.rem(i, heads)
        other = jnp.logical_or(group != own_group, owner_of(index, heads, seq) != own_seq)

        @pl.when(other)
        def _():
            for array in range(4):
                pltpu.make_async_remote_copy(
                    src_ref=part(0, array),
                    dst_ref=column(group, index, array),
                    send_sem=send_sem.at[array, 0],
                    recv_sem=recv_sem.at[array, group * heads + index],
                    device_id=(owner_of(index, heads, seq), group),
                    device_id_type=MESH,
                ).wait_recv()

        return carry

    def text_arrive(index, carry):
        @pl.when(owner_of(index, heads, seq) != own_seq)
        def _():
            for array in range(4):
                text_remote(text_in[array], index, array, owner_of(index, heads, seq)).wait_recv()
            pl.when(relays(index))(
                lambda: text_beside(
                    lambda copy: copy.start(), index, lambda array: text_column(index, array)
                )
            )

        return carry

    def relays(index):
        owner = owner_of(index, heads, seq)
        return jnp.logical_and(owner != own_seq, owner % cores == own_seq % cores)

    def text_relayed(index, carry):
        pl.when(relays(index))(
            lambda: text_beside(
                lambda copy: copy.wait_send(), index, lambda array: text_column(index, array)
            )
        )
        return carry

    lax.fori_loop(0, heads, text_arrive, 0)
    lax.fori_loop(0, head * heads, arrive, 0)
    lax.fori_loop(0, heads, text_relayed, 0)

    @pl.when(mine)
    def _():
        each(lambda copy: copy.wait_send())
        for array in range(4):
            local(array).wait()
            text_local(array).wait()


def scatter_heads(seq, head, heads, video, texts):
    rows = video[0].shape[0] // (seq * head)
    text = texts[0].shape[0]
    return pl.pallas_call(
        functools.partial(scatter_kernel, seq, head, heads),
        in_specs=[pl.BlockSpec(memory_space=pl.ANY)] * 8,
        out_specs=[pl.BlockSpec(memory_space=pl.ANY)] * 8,
        out_shape=[jax.ShapeDtypeStruct((rows, head * heads * HD), jnp.bfloat16)] * 4
        + [jax.ShapeDtypeStruct((text, heads * HD), jnp.bfloat16)] * 4,
        scratch_shapes=[
            pltpu.SemaphoreType.DMA((4, seq * head)),
            pltpu.SemaphoreType.DMA((4, head * heads)),
            pltpu.SemaphoreType.DMA((4,)),
            pltpu.SemaphoreType.DMA((4, heads, seq)),
            pltpu.SemaphoreType.DMA((4, heads)),
            pltpu.SemaphoreType.DMA((4,)),
        ],
        compiler_params=pltpu.CompilerParams(collective_id=1, has_side_effects=True),
        name="scatter_heads",
    )(*video, *texts)


def settle_kernel(*refs):
    for source, result in zip(refs[:8], refs[8:]):
        result[...] = source[...]


def settle(arrays):
    steps = 4
    specs = [pl.BlockSpec((x.shape[0] // steps, x.shape[1]), lambda i: (i, 0)) for x in arrays]
    return pl.pallas_call(
        settle_kernel,
        grid=(steps,),
        in_specs=specs,
        out_specs=specs,
        out_shape=[jax.ShapeDtypeStruct(x.shape, x.dtype) for x in arrays],
        name="settle",
    )(*arrays)


def text_pass(refs):
    (k_ref, v_ref, tq_ref, tg_ref, tk_ref, tv_ref, bias_ref, to_ref, tdq_ref, sbuf, dk_acc, dv_acc) = refs
    video = k_ref.shape[0]
    text = tk_ref.shape[0]
    scale2 = FACTOR * LOG2E
    block = 512
    steps = video // block
    tq = tq_ref[...]
    tg = tg_ref[...]
    text_s = dot_nt(tk_ref[...], tq) * scale2 + bias_ref[:, :1]
    top = jnp.max(text_s, axis=0, keepdims=True)

    def scores(i, top):
        rows = pl.ds(pl.multiple_of(i * block, block), block)
        s = dot_nt(k_ref[rows, :], tq) * scale2
        sbuf[rows, :] = s
        return jnp.maximum(top, jnp.max(s, axis=0, keepdims=True))

    top = lax.fori_loop(0, steps, scores, top)
    text_e = jnp.exp2(text_s - top)

    def weigh(i, carry):
        total, out = carry
        rows = pl.ds(pl.multiple_of(i * block, block), block)
        e = jnp.exp2(sbuf[rows, :] - top)
        sbuf[rows, :] = e
        out = out + dot_tn(e.astype(jnp.bfloat16), v_ref[rows, :])
        return total + jnp.sum(e, axis=0, keepdims=True), out

    total, out = lax.fori_loop(
        0,
        steps,
        weigh,
        (
            jnp.sum(text_e, axis=0, keepdims=True),
            dot_tn(text_e.astype(jnp.bfloat16), tv_ref[...]),
        ),
    )
    inverse = 1.0 / total
    out = out * jnp.transpose(inverse)
    to_ref[...] = out.astype(jnp.bfloat16)
    delta = jnp.transpose(jnp.sum(tg.astype(jnp.float32) * out, axis=1, keepdims=True))

    def spread(e, key, value):
        p = e * inverse
        dv = dot_nn(p.astype(jnp.bfloat16), tg)
        ds = (p * (dot_nt(value, tg) - delta)).astype(jnp.bfloat16)
        return dot_nn(ds, tq), dv, dot_tn(ds, key)

    dk, dv, dq = spread(text_e, tk_ref[...], tv_ref[...])
    dk_acc[pl.ds(video, text), :] = dk
    dv_acc[pl.ds(video, text), :] = dv

    def back(i, dq):
        rows = pl.ds(pl.multiple_of(i * block, block), block)
        dk, dv, more = spread(sbuf[rows, :], k_ref[rows, :], v_ref[rows, :])
        dk_acc[rows, :] = dk
        dv_acc[rows, :] = dv
        return dq + more

    dq = lax.fori_loop(0, steps, back, dq)
    tdq_ref[...] = (dq * FACTOR).astype(jnp.bfloat16)


def attend_kernel(
    entries,
    own_ref,
    slot_ref,
    count_ref,
    q_ref,
    g_ref,
    k_ref,
    v_ref,
    tq_ref,
    tg_ref,
    tk_ref,
    tv_ref,
    bias_ref,
    o_ref,
    dq_ref,
    dk_ref,
    dv_ref,
    to_ref,
    tdq_ref,
    tdk_ref,
    tdv_ref,
    kbuf,
    vbuf,
    sbuf,
    dk_acc,
    dv_acc,
):
    video = k_ref.shape[0]
    text = tk_ref.shape[0]
    chunk = q_ref.shape[0]
    scale2 = FACTOR * LOG2E
    step = pl.program_id(0)
    active = own_ref[1] > 0

    @pl.when(jnp.logical_and(active, step == 0))
    def _():
        kbuf[pl.ds(0, text), :] = tk_ref[...]
        vbuf[pl.ds(0, text), :] = tv_ref[...]
        text_pass(
            (k_ref, v_ref, tq_ref, tg_ref, tk_ref, tv_ref, bias_ref, to_ref, tdq_ref, sbuf, dk_acc, dv_acc)
        )

    def tile_of(i, used):
        rows = pl.ds(pl.multiple_of(i * TILE, TILE), TILE)
        number = step * (chunk // TILE) + i
        spots = [
            pl.ds(pl.multiple_of(slot_ref[number * entries + e] * TILE, TILE), TILE)
            for e in range(used)
        ]
        q = q_ref[rows, :]
        g = g_ref[rows, :]
        for e in range(used):
            kbuf[pl.ds(text + e * TILE, TILE), :] = k_ref[spots[e], :]
            vbuf[pl.ds(text + e * TILE, TILE), :] = v_ref[spots[e], :]
        keys = kbuf[pl.ds(0, text + used * TILE), :]
        values = vbuf[pl.ds(0, text + used * TILE), :]
        s = dot_nt(keys, q) * scale2
        s = jnp.concatenate([s[:text] + bias_ref[...], s[text:]], axis=0)
        e = jnp.exp2(s - jnp.max(s, axis=0, keepdims=True))
        p = e * (1.0 / jnp.sum(e, axis=0, keepdims=True))
        weights = p.astype(jnp.bfloat16)
        o_ref[rows, :] = dot_tn(weights, values).astype(jnp.bfloat16)
        pull = p * dot_nt(values, g)
        ds = (pull - p * jnp.sum(pull, axis=0, keepdims=True)).astype(jnp.bfloat16)
        dq_ref[rows, :] = (dot_tn(ds, keys) * FACTOR).astype(jnp.bfloat16)
        dk = dot_nn(ds, q)
        dv = dot_nn(weights, g)
        for e in range(used):
            at = text + e * TILE
            dk_acc[spots[e], :] += dk[at : at + TILE]
            dv_acc[spots[e], :] += dv[at : at + TILE]
        dk_acc[pl.ds(video, text), :] += dk[:text]
        dv_acc[pl.ds(video, text), :] += dv[:text]

    def tile(i, carry):
        count = count_ref[step * (chunk // TILE) + i]
        for used in range(1, entries + 1):
            pl.when(count == used)(functools.partial(tile_of, i, used))
        return carry

    @pl.when(active)
    def _():
        lax.fori_loop(0, chunk // TILE, tile, 0)

    @pl.when(jnp.logical_and(active, step == pl.num_programs(0) - 1))
    def _():
        dk_ref[...] = (dk_acc[pl.ds(0, video), :] * FACTOR).astype(dk_ref.dtype)
        dv_ref[...] = dv_acc[pl.ds(0, video), :].astype(dv_ref.dtype)
        tdk_ref[...] = (dk_acc[pl.ds(video, text), :] * FACTOR).astype(tdk_ref.dtype)
        tdv_ref[...] = dv_acc[pl.ds(video, text), :].astype(tdv_ref.dtype)


def attend(own, slots, counts, q, g, k, v, tq, tg, tk, tv, bias):
    video = k.shape[0]
    text = tk.shape[0]
    entries = slots.shape[1]
    chunk = min(video, 1024)
    total = video + text
    block = pl.BlockSpec((chunk, HD), lambda i, *_: (i, 0))
    held = pl.BlockSpec((video, HD), lambda i, *_: (0, 0), pipeline_mode=pl.Buffered(1))
    given = pl.BlockSpec((text, HD), lambda i, own, *_: (0, own[0]))
    made = pl.BlockSpec((text, HD), lambda i, *_: (0, 0))
    whole = pl.BlockSpec((video, HD), lambda i, *_: (0, 0))
    video_shape = jax.ShapeDtypeStruct((video, HD), jnp.bfloat16)
    text_shape = jax.ShapeDtypeStruct((text, HD), jnp.bfloat16)
    call = pl.pallas_call(
        functools.partial(attend_kernel, entries),
        grid_spec=pltpu.PrefetchScalarGridSpec(
            num_scalar_prefetch=3,
            grid=(video // chunk,),
            in_specs=[block, block, held, held, given, given, given, given, made],
            out_specs=[block, block, whole, whole, made, made, made, made],
            scratch_shapes=[
                pltpu.VMEM((entries * TILE + text, HD), jnp.bfloat16),
                pltpu.VMEM((entries * TILE + text, HD), jnp.bfloat16),
                pltpu.VMEM((video, text), jnp.float32),
                pltpu.VMEM((total, HD), jnp.float32),
                pltpu.VMEM((total, HD), jnp.float32),
            ],
        ),
        out_shape=[video_shape] * 4 + [text_shape] * 4,
        compiler_params=pltpu.CompilerParams(vmem_limit_bytes=63 * 1024 * 1024),
        name="attend",
    )
    return call(own, slots.reshape(-1), counts, q, g, k, v, tq, tg, tk, tv, bias)


def body(
    video_query,
    video_key,
    video_value,
    video_grad,
    text_query,
    text_key,
    text_value,
    text_grad,
    tile_list,
    tile_count,
    text_mask,
):
    seq, head = lax.axis_size("seq"), lax.axis_size("head")
    text, width = text_query.shape
    heads = width // HD
    keys, values, queries, grads = gather_heads(
        seq, head, heads, (video_key, video_value, video_query, video_grad)
    )
    index, mine = own_head(heads, seq)
    own = jnp.stack([index, mine.astype(jnp.int32)]).astype(jnp.int32)
    bias = jnp.broadcast_to(
        jnp.where(text_mask > 0, 0.0, NEGATIVE).astype(jnp.float32)[:, None], (text, HD)
    )
    o, dq, dk, dv, to, tdq, tdk, tdv = attend(
        own,
        tile_list,
        tile_count,
        queries,
        grads,
        keys,
        values,
        text_query,
        text_grad,
        text_key,
        text_value,
        bias,
    )
    return tuple(settle(scatter_heads(seq, head, heads, (o, dq, dk, dv), (to, tdq, tdk, tdv))))


def solution(mesh):
    video = P(("seq", "head"), None)
    side = P(None, "head")
    return jax.shard_map(
        body,
        mesh=mesh,
        in_specs=(video,) * 4 + (side,) * 4 + (P(), P(), P()),
        out_specs=(video,) * 4 + (side,) * 4,
        check_vma=False,
    )
```

```python
import functools

import jax
import jax.numpy as jnp
from jax import lax
from jax.experimental import pallas as pl
from jax.experimental.pallas import tpu as pltpu
from jax.sharding import PartitionSpec as P

HD = 128
TILE = 128
NEGATIVE = -1e30
LOG2E = 1.4426950408889634
FACTOR = HD**-0.5


def dot_nt(a, b):
    return lax.dot_general(a, b, (((1,), (1,)), ((), ())), preferred_element_type=jnp.float32)


def dot_tn(a, b):
    return lax.dot_general(a, b, (((0,), (0,)), ((), ())), preferred_element_type=jnp.float32)


def dot_nn(a, b):
    return lax.dot_general(a, b, (((1,), (0,)), ((), ())), preferred_element_type=jnp.float32)


MESH = pl.DeviceIdType.MESH


def owner_of(index, heads, seq):
    return (index * seq) // heads


def own_head(heads, seq):
    place = lax.axis_index("seq")
    index = (place * heads + seq - 1) // seq
    mine = jnp.logical_and(index < heads, owner_of(index, heads, seq) == place)
    return jnp.minimum(index, heads - 1), mine


def greet(seq, head):
    own_seq, own_group = lax.axis_index("seq"), lax.axis_index("head")
    barrier = pltpu.get_barrier_semaphore()

    def signal(i, carry):
        at = lax.rem(own_seq * head + own_group + i, seq * head)
        pl.semaphore_signal(barrier, inc=1, device_id=(at // head, lax.rem(at, head)), device_id_type=MESH)
        return carry

    lax.fori_loop(1, seq * head, signal, 0)
    pl.semaphore_wait(barrier, seq * head - 1)


def gather_kernel(seq, head, heads, *refs):
    count = 4
    ins, outs = refs[:count], refs[count : 2 * count]
    send_sem, recv_sem, own_sem = refs[2 * count :]
    own_seq, own_group = lax.axis_index("seq"), lax.axis_index("head")
    me = own_seq * head + own_group
    rows = ins[0].shape[0]
    mine_index, mine = own_head(heads, seq)
    greet(seq, head)
    total = head * heads

    def piece(group, index, array):
        column = pl.multiple_of((group * heads + index) * HD, HD)
        return ins[array].at[:, pl.ds(column, HD)]

    def place(device, array):
        return outs[array].at[pl.ds(pl.multiple_of(device * rows, rows), rows), :]

    def remote(group, index, array):
        return pltpu.make_async_remote_copy(
            src_ref=piece(group, index, array),
            dst_ref=place(me, array),
            send_sem=send_sem.at[array, group * heads + index],
            recv_sem=recv_sem.at[array, me],
            device_id=(owner_of(index, heads, seq), group),
            device_id_type=MESH,
        )

    def local(array):
        return pltpu.make_async_copy(
            piece(own_group, mine_index, array), place(me, array), own_sem.at[array]
        )

    def each_target(act):
        def step(i, carry):
            group = lax.rem(own_group + lax.rem(i, head), head)
            index = lax.rem(i // head + own_seq, heads)
            other = jnp.logical_or(group != own_group, owner_of(index, heads, seq) != own_seq)

            @pl.when(other)
            def _():
                for array in range(count):
                    act(remote(group, index, array))

            return carry

        lax.fori_loop(0, total, step, 0)

    each_target(lambda copy: copy.start())

    @pl.when(mine)
    def _():
        for array in range(count):
            local(array).start()

        def arrive(i, carry):
            source = lax.rem(me + i, seq * head)
            for array in range(count):
                pltpu.make_async_remote_copy(
                    src_ref=piece(own_group, mine_index, array),
                    dst_ref=place(source, array),
                    send_sem=send_sem.at[array, 0],
                    recv_sem=recv_sem.at[array, source],
                    device_id=(source // head, lax.rem(source, head)),
                    device_id_type=MESH,
                ).wait_recv()
            return carry

        lax.fori_loop(1, seq * head, arrive, 0)
        for array in range(count):
            local(array).wait()

    each_target(lambda copy: copy.wait_send())


def gather_heads(seq, head, heads, arrays):
    rows = arrays[0].shape[0] * seq * head
    return pl.pallas_call(
        functools.partial(gather_kernel, seq, head, heads),
        in_specs=[pl.BlockSpec(memory_space=pl.ANY)] * 4,
        out_specs=[pl.BlockSpec(memory_space=pl.ANY)] * 4,
        out_shape=[jax.ShapeDtypeStruct((rows, HD), jnp.bfloat16)] * 4,
        scratch_shapes=[
            pltpu.SemaphoreType.DMA((4, head * heads)),
            pltpu.SemaphoreType.DMA((4, seq * head)),
            pltpu.SemaphoreType.DMA((4,)),
        ],
        compiler_params=pltpu.CompilerParams(collective_id=0, has_side_effects=True),
        name="gather_heads",
    )(*arrays)


def scatter_kernel(seq, head, heads, *refs):
    video_in, text_in, video_out, text_out = refs[:4], refs[4:8], refs[8:12], refs[12:16]
    send_sem, recv_sem, own_sem, text_send, text_recv, text_own = refs[16:]
    own_seq, own_group = lax.axis_index("seq"), lax.axis_index("head")
    me = own_seq * head + own_group
    rows = video_out[0].shape[0]
    mine_index, mine = own_head(heads, seq)
    cores = 2 if seq % 2 == 0 else 1
    greet(seq, head)

    def part(device, array):
        return video_in[array].at[pl.ds(pl.multiple_of(device * rows, rows), rows), :]

    def column(group, index, array):
        at = pl.multiple_of((group * heads + index) * HD, HD)
        return video_out[array].at[:, pl.ds(at, HD)]

    def text_column(index, array):
        return text_out[array].at[:, pl.ds(pl.multiple_of(index * HD, HD), HD)]

    def remote(device, array):
        return pltpu.make_async_remote_copy(
            src_ref=part(device, array),
            dst_ref=column(own_group, mine_index, array),
            send_sem=send_sem.at[array, device],
            recv_sem=recv_sem.at[array, own_group * heads + mine_index],
            device_id=(device // head, lax.rem(device, head)),
            device_id_type=MESH,
        )

    def text_remote(source, index, array, place):
        return pltpu.make_async_remote_copy(
            src_ref=source,
            dst_ref=text_column(index, array),
            send_sem=text_send.at[array, index, place],
            recv_sem=text_recv.at[array, index],
            device_id=(place, own_group),
            device_id_type=MESH,
        )

    def text_beside(act, index, sources):
        if cores == 2:
            for array in range(4):
                act(text_remote(sources(array), index, array, own_seq + 1 - 2 * (own_seq % 2)))

    def text_far(act, index, sources):
        def step(i, carry):
            for array in range(4):
                act(text_remote(sources(array), index, array, lax.rem(own_seq + i * cores, seq)))
            return carry

        lax.fori_loop(1, seq // cores, step, 0)

    def local(array):
        return pltpu.make_async_copy(
            part(me, array), column(own_group, mine_index, array), own_sem.at[array]
        )

    def text_local(array):
        return pltpu.make_async_copy(
            text_in[array], text_column(mine_index, array), text_own.at[array]
        )

    def each(act):
        def step(i, carry):
            for array in range(4):
                place = lax.rem(own_seq + i // head, seq)
                act(remote(place * head + lax.rem(own_group + lax.rem(i, head), head), array))
            return carry

        text_far(act, mine_index, lambda array: text_in[array])
        text_beside(act, mine_index, lambda array: text_in[array])
        lax.fori_loop(1, seq * head, step, 0)

    @pl.when(mine)
    def _():
        each(lambda copy: copy.start())
        for array in range(4):
            local(array).start()
            text_local(array).start()

    def arrive(i, carry):
        group = i // heads
        index = lax.rem(i, heads)
        other = jnp.logical_or(group != own_group, owner_of(index, heads, seq) != own_seq)

        @pl.when(other)
        def _():
            for array in range(4):
                pltpu.make_async_remote_copy(
                    src_ref=part(0, array),
                    dst_ref=column(group, index, array),
                    send_sem=send_sem.at[array, 0],
                    recv_sem=recv_sem.at[array, group * heads + index],
                    device_id=(owner_of(index, heads, seq), group),
                    device_id_type=MESH,
                ).wait_recv()

        return carry

    def text_arrive(index, carry):
        @pl.when(owner_of(index, heads, seq) != own_seq)
        def _():
            for array in range(4):
                text_remote(text_in[array], index, array, owner_of(index, heads, seq)).wait_recv()
            pl.when(relays(index))(
                lambda: text_beside(
                    lambda copy: copy.start(), index, lambda array: text_column(index, array)
                )
            )

        return carry

    def relays(index):
        owner = owner_of(index, heads, seq)
        return jnp.logical_and(owner != own_seq, owner % cores == own_seq % cores)

    def text_relayed(index, carry):
        pl.when(relays(index))(
            lambda: text_beside(
                lambda copy: copy.wait_send(), index, lambda array: text_column(index, array)
            )
        )
        return carry

    lax.fori_loop(0, heads, text_arrive, 0)
    lax.fori_loop(0, head * heads, arrive, 0)
    lax.fori_loop(0, heads, text_relayed, 0)

    @pl.when(mine)
    def _():
        each(lambda copy: copy.wait_send())
        for array in range(4):
            local(array).wait()
            text_local(array).wait()


def scatter_heads(seq, head, heads, video, texts):
    rows = video[0].shape[0] // (seq * head)
    text = texts[0].shape[0]
    return pl.pallas_call(
        functools.partial(scatter_kernel, seq, head, heads),
        in_specs=[pl.BlockSpec(memory_space=pl.ANY)] * 8,
        out_specs=[pl.BlockSpec(memory_space=pl.ANY)] * 8,
        out_shape=[jax.ShapeDtypeStruct((rows, head * heads * HD), jnp.bfloat16)] * 4
        + [jax.ShapeDtypeStruct((text, heads * HD), jnp.bfloat16)] * 4,
        scratch_shapes=[
            pltpu.SemaphoreType.DMA((4, seq * head)),
            pltpu.SemaphoreType.DMA((4, head * heads)),
            pltpu.SemaphoreType.DMA((4,)),
            pltpu.SemaphoreType.DMA((4, heads, seq)),
            pltpu.SemaphoreType.DMA((4, heads)),
            pltpu.SemaphoreType.DMA((4,)),
        ],
        compiler_params=pltpu.CompilerParams(collective_id=1, has_side_effects=True),
        name="scatter_heads",
    )(*video, *texts)


def settle_kernel(*refs):
    for source, result in zip(refs[:8], refs[8:]):
        result[...] = source[...]


def settle(arrays):
    steps = 4
    specs = [pl.BlockSpec((x.shape[0] // steps, x.shape[1]), lambda i: (i, 0)) for x in arrays]
    return pl.pallas_call(
        settle_kernel,
        grid=(steps,),
        in_specs=specs,
        out_specs=specs,
        out_shape=[jax.ShapeDtypeStruct(x.shape, x.dtype) for x in arrays],
        name="settle",
    )(*arrays)


def text_pass(refs):
    (k_ref, v_ref, tq_ref, tg_ref, tk_ref, tv_ref, bias_ref, to_ref, tdq_ref, sbuf, dk_acc, dv_acc) = refs
    video = k_ref.shape[0]
    text = tk_ref.shape[0]
    scale2 = FACTOR * LOG2E
    block = 512
    steps = video // block
    tq = tq_ref[...]
    tg = tg_ref[...]
    text_s = dot_nt(tk_ref[...], tq) * scale2 + bias_ref[:, :1]
    top = jnp.max(text_s, axis=0, keepdims=True)

    def scores(i, top):
        rows = pl.ds(pl.multiple_of(i * block, block), block)
        s = dot_nt(k_ref[rows, :], tq) * scale2
        sbuf[rows, :] = s
        return jnp.maximum(top, jnp.max(s, axis=0, keepdims=True))

    top = lax.fori_loop(0, steps, scores, top)
    text_e = jnp.exp2(text_s - top)

    def weigh(i, carry):
        total, out = carry
        rows = pl.ds(pl.multiple_of(i * block, block), block)
        e = jnp.exp2(sbuf[rows, :] - top)
        sbuf[rows, :] = e
        out = out + dot_tn(e.astype(jnp.bfloat16), v_ref[rows, :])
        return total + jnp.sum(e, axis=0, keepdims=True), out

    total, out = lax.fori_loop(
        0,
        steps,
        weigh,
        (
            jnp.sum(text_e, axis=0, keepdims=True),
            dot_tn(text_e.astype(jnp.bfloat16), tv_ref[...]),
        ),
    )
    inverse = 1.0 / total
    out = out * jnp.transpose(inverse)
    to_ref[...] = out.astype(jnp.bfloat16)
    delta = jnp.transpose(jnp.sum(tg.astype(jnp.float32) * out, axis=1, keepdims=True))

    def spread(e, key, value):
        p = e * inverse
        dv = dot_nn(p.astype(jnp.bfloat16), tg)
        ds = (p * (dot_nt(value, tg) - delta)).astype(jnp.bfloat16)
        return dot_nn(ds, tq), dv, dot_tn(ds, key)

    dk, dv, dq = spread(text_e, tk_ref[...], tv_ref[...])
    dk_acc[pl.ds(video, text), :] = dk
    dv_acc[pl.ds(video, text), :] = dv

    def back(i, dq):
        rows = pl.ds(pl.multiple_of(i * block, block), block)
        dk, dv, more = spread(sbuf[rows, :], k_ref[rows, :], v_ref[rows, :])
        dk_acc[rows, :] = dk
        dv_acc[rows, :] = dv
        return dq + more

    dq = lax.fori_loop(0, steps, back, dq)
    tdq_ref[...] = (dq * FACTOR).astype(jnp.bfloat16)


def attend_kernel(
    entries,
    own_ref,
    slot_ref,
    count_ref,
    q_ref,
    g_ref,
    k_ref,
    v_ref,
    tq_ref,
    tg_ref,
    tk_ref,
    tv_ref,
    bias_ref,
    o_ref,
    dq_ref,
    dk_ref,
    dv_ref,
    to_ref,
    tdq_ref,
    tdk_ref,
    tdv_ref,
    kbuf,
    vbuf,
    sbuf,
    dk_acc,
    dv_acc,
):
    video = k_ref.shape[0]
    text = tk_ref.shape[0]
    chunk = q_ref.shape[0]
    scale2 = FACTOR * LOG2E
    step = pl.program_id(0)
    active = own_ref[1] > 0

    @pl.when(jnp.logical_and(active, step == 0))
    def _():
        kbuf[pl.ds(0, text), :] = tk_ref[...]
        vbuf[pl.ds(0, text), :] = tv_ref[...]
        text_pass(
            (k_ref, v_ref, tq_ref, tg_ref, tk_ref, tv_ref, bias_ref, to_ref, tdq_ref, sbuf, dk_acc, dv_acc)
        )

    def tile_of(i, used):
        rows = pl.ds(pl.multiple_of(i * TILE, TILE), TILE)
        number = step * (chunk // TILE) + i
        spots = [
            pl.ds(pl.multiple_of(slot_ref[number * entries + e] * TILE, TILE), TILE)
            for e in range(used)
        ]
        q = q_ref[rows, :]
        g = g_ref[rows, :]
        for e in range(used):
            kbuf[pl.ds(text + e * TILE, TILE), :] = k_ref[spots[e], :]
            vbuf[pl.ds(text + e * TILE, TILE), :] = v_ref[spots[e], :]
        keys = kbuf[pl.ds(0, text + used * TILE), :]
        values = vbuf[pl.ds(0, text + used * TILE), :]
        s = dot_nt(keys, q) * scale2
        s = jnp.concatenate([s[:text] + bias_ref[...], s[text:]], axis=0)
        e = jnp.exp2(s - jnp.max(s, axis=0, keepdims=True))
        p = e * (1.0 / jnp.sum(e, axis=0, keepdims=True))
        weights = p.astype(jnp.bfloat16)
        o_ref[rows, :] = dot_tn(weights, values).astype(jnp.bfloat16)
        pull = p * dot_nt(values, g)
        ds = (pull - p * jnp.sum(pull, axis=0, keepdims=True)).astype(jnp.bfloat16)
        dq_ref[rows, :] = (dot_tn(ds, keys) * FACTOR).astype(jnp.bfloat16)
        dk = dot_nn(ds, q)
        dv = dot_nn(weights, g)
        for e in range(used):
            at = text + e * TILE
            dk_acc[spots[e], :] += dk[at : at + TILE]
            dv_acc[spots[e], :] += dv[at : at + TILE]
        dk_acc[pl.ds(video, text), :] += dk[:text]
        dv_acc[pl.ds(video, text), :] += dv[:text]

    def tile(i, carry):
        count = count_ref[step * (chunk // TILE) + i]
        for used in range(1, entries + 1):
            pl.when(count == used)(functools.partial(tile_of, i, used))
        return carry

    @pl.when(active)
    def _():
        lax.fori_loop(0, chunk // TILE, tile, 0)

    @pl.when(jnp.logical_and(active, step == pl.num_programs(0) - 1))
    def _():
        dk_ref[...] = (dk_acc[pl.ds(0, video), :] * FACTOR).astype(dk_ref.dtype)
        dv_ref[...] = dv_acc[pl.ds(0, video), :].astype(dv_ref.dtype)
        tdk_ref[...] = (dk_acc[pl.ds(video, text), :] * FACTOR).astype(tdk_ref.dtype)
        tdv_ref[...] = dv_acc[pl.ds(video, text), :].astype(tdv_ref.dtype)


def attend(own, slots, counts, q, g, k, v, tq, tg, tk, tv, bias):
    video = k.shape[0]
    text = tk.shape[0]
    entries = slots.shape[1]
    chunk = min(video, 1024)
    total = video + text
    block = pl.BlockSpec((chunk, HD), lambda i, *_: (i, 0))
    held = pl.BlockSpec((video, HD), lambda i, *_: (0, 0), pipeline_mode=pl.Buffered(1))
    given = pl.BlockSpec((text, HD), lambda i, own, *_: (0, own[0]))
    made = pl.BlockSpec((text, HD), lambda i, *_: (0, 0))
    whole = pl.BlockSpec((video, HD), lambda i, *_: (0, 0))
    video_shape = jax.ShapeDtypeStruct((video, HD), jnp.bfloat16)
    text_shape = jax.ShapeDtypeStruct((text, HD), jnp.bfloat16)
    call = pl.pallas_call(
        functools.partial(attend_kernel, entries),
        grid_spec=pltpu.PrefetchScalarGridSpec(
            num_scalar_prefetch=3,
            grid=(video // chunk,),
            in_specs=[block, block, held, held, given, given, given, given, made],
            out_specs=[block, block, whole, whole, made, made, made, made],
            scratch_shapes=[
                pltpu.VMEM((entries * TILE + text, HD), jnp.bfloat16),
                pltpu.VMEM((entries * TILE + text, HD), jnp.bfloat16),
                pltpu.VMEM((video, text), jnp.float32),
                pltpu.VMEM((total, HD), jnp.float32),
                pltpu.VMEM((total, HD), jnp.float32),
            ],
        ),
        out_shape=[video_shape] * 4 + [text_shape] * 4,
        compiler_params=pltpu.CompilerParams(vmem_limit_bytes=63 * 1024 * 1024),
        name="attend",
    )
    return call(own, slots.reshape(-1), counts, q, g, k, v, tq, tg, tk, tv, bias)


def body(
    video_query,
    video_key,
    video_value,
    video_grad,
    text_query,
    text_key,
    text_value,
    text_grad,
    tile_list,
    tile_count,
    text_mask,
):
    seq, head = lax.axis_size("seq"), lax.axis_size("head")
    text, width = text_query.shape
    heads = width // HD
    keys, values, queries, grads = gather_heads(
        seq, head, heads, (video_key, video_value, video_query, video_grad)
    )
    index, mine = own_head(heads, seq)
    own = jnp.stack([index, mine.astype(jnp.int32)]).astype(jnp.int32)
    bias = jnp.broadcast_to(
        jnp.where(text_mask > 0, 0.0, NEGATIVE).astype(jnp.float32)[:, None], (text, HD)
    )
    o, dq, dk, dv, to, tdq, tdk, tdv = attend(
        own,
        tile_list,
        tile_count,
        queries,
        grads,
        keys,
        values,
        text_query,
        text_grad,
        text_key,
        text_value,
        bias,
    )
    return tuple(settle(scatter_heads(seq, head, heads, (o, dq, dk, dv), (to, tdq, tdk, tdv))))


def solution(mesh):
    video = P(("seq", "head"), None)
    side = P(None, "head")
    return jax.shard_map(
        body,
        mesh=mesh,
        in_specs=(video,) * 4 + (side,) * 4 + (P(), P(), P()),
        out_specs=(video,) * 4 + (side,) * 4,
        check_vma=False,
    )
```
